32 devices in a mesh: fsdp: 8 (over z, y), ctx: 2 (over x), tp: 2 (over core).
Axes of the slice: x: 2, y: 2, z: 4, core: 2. Of those that a mesh axis runs over, the one named last changes fastest.
Arguments:
- inputs: bfloat16 [8, 1024, 2048], P('fsdp', 'ctx'), may hold values from -6 to 6
- gain_attn: bfloat16 [2048], P('fsdp'), may hold values from 0.5 to 1.5
- w_query: bfloat16 [2048, 2048], P('fsdp', 'tp'), may hold values from -0.03125 to 0.03125
- w_key: bfloat16 [2048, 2048], P('fsdp', 'tp'), may hold values from -0.125 to 0.125
- w_value: bfloat16 [2048, 2048], P('fsdp', 'tp'), may hold values from -0.125 to 0.125
- w_out: bfloat16 [2048, 2048], P('fsdp', 'tp'), may hold values from -0.25 to 0.25
- bias_table: bfloat16 [32, 32], P(None, 'tp'), may hold values from -3 to 3
- buckets: int32 [2047], replicated, may hold values from 0 to 31
- gain_ffn: bfloat16 [2048], P('fsdp'), may hold values from 0.5 to 1.5
- w_gate: bfloat16 [2048, 5120], P('fsdp', 'tp'), may hold values from -0.125 to 0.125
- w_up: bfloat16 [2048, 5120], P('fsdp', 'tp'), may hold values from -0.125 to 0.125
- w_down: bfloat16 [2048, 5120], P('fsdp', 'tp'), may hold values from -0.078125 to 0.078125
- cotangent: bfloat16 [8, 1024, 2048], P('fsdp', 'ctx'), may hold values from -6 to 6
Outputs:
- output: bfloat16 [8, 1024, 2048], P('fsdp', 'ctx')
- input_grad: bfloat16 [8, 1024, 2048], P('fsdp', 'ctx')
- gain_attn_grad: float32 [2048], P(('fsdp', 'ctx'))
- query_grad: float32 [2048, 2048], P(('fsdp', 'ctx'), 'tp')
- key_grad: float32 [2048, 2048], P(('fsdp', 'ctx'), 'tp')
- value_grad: float32 [2048, 2048], P(('fsdp', 'ctx'), 'tp')
- out_grad: float32 [2048, 2048], P(('fsdp', 'ctx'), 'tp')
- table_grad: float32 [32, 32], P(None, 'tp')
- gain_ffn_grad: float32 [2048], P(('fsdp', 'ctx'))
- gate_grad: float32 [2048, 5120], P(('fsdp', 'ctx'), 'tp')
- up_grad: float32 [2048, 5120], P(('fsdp', 'ctx'), 'tp')
- down_grad: float32 [2048, 5120], P(('fsdp', 'ctx'), 'tp')
The draws below stay inside these ranges and needn't reach their ends.
All inputs are finite; a program needn't handle non-finite values.
Results may differ from the reference program's by a relative error of at most 0.018.
Values may be sent and summed in bfloat16 or wider, within the bound.
No kernel may reach another device: no remote copies, remote signals or barrier semaphores. Data moves between devices by JAX's collectives and lax.ppermute only.
A program may use at most 256 MiB of HBM per device.

```python
from functools import partial
import jax
import jax.numpy as jnp
from jax import lax

D = 2048
H = 32
DH = 64
FF = 5120
BUCKETS = 32
LEN = 1024
HD = 2048
SEQS = 8


def set_ends(values, rng, smallest, high):
    longest = values.shape.index(max(values.shape))
    spots = []
    for shift in (0, 1):
        where = [jax.random.randint(jax.random.fold_in(rng, axis), (), 0, length) for axis, length in enumerate(values.shape)]
        where[longest] = (where[longest] + shift) % values.shape[longest]
        spots.append(tuple(where))
    return values.at[spots[0]].set(smallest).at[spots[1]].set(high)


def with_spikes(entries, stream_key, source, target, blocks, factor):
    owner, partner = [(jnp.arange(entries.shape[position]) // (entries.shape[position] // blocks)).reshape([-1 if axis == position else 1 for axis in range(entries.ndim)]) for position in (source, target)]
    chosen = jax.random.permutation(stream_key, blocks)[partner]
    strong = (owner == chosen) | (owner == (partner + blocks // 2) % blocks)
    return jnp.where(strong, factor * entries, entries)


def shard_levels(rng, extent, split, low, top_value):
    def one(position, blocks):
        draws = jax.random.uniform(jax.random.fold_in(jax.random.fold_in(rng, 6), position), (blocks,), jnp.float32, low / len(split), top_value / len(split))
        return jnp.repeat(jnp.exp(draws), extent[position] // blocks).reshape((-1,) + (1,) * (len(extent) - position - 1))

    loudness = one(*split[0])
    for cut in split[1:]:
        loudness = loudness * one(*cut)
    return loudness


def scatter_about(own_key, extent, width, most, shards=(), held_as=jnp.bfloat16):
    factor_of = shard_levels(own_key, extent, shards, -0.22, 0.18) if shards else 1.0
    array = jax.random.normal(own_key, extent, jnp.float32) * width * factor_of
    return jnp.minimum(jnp.maximum(array, -most), most).astype(held_as)


def noise_with(stream_key, shape, scale, most, cuts, heavy, held_as=jnp.bfloat16):
    values = scale * jax.random.normal(stream_key, shape, jnp.float32)
    if cuts:
        values = values * shard_levels(stream_key, shape, cuts, -0.22, 0.18)
    return jnp.clip(with_spikes(values, jax.random.fold_in(stream_key, 3), *heavy), -most, most).astype(held_as)


def setup_inputs(seed: int = 0) -> dict:
    arg_keys = jax.random.split(jax.random.key(seed), 14)
    inputs = scatter_about(arg_keys[0], (SEQS, LEN, D), 1.0, 6.0, ((0, 8), (1, 2)))
    gain_attn = jnp.clip(1.0 + 0.1 * jax.random.normal(arg_keys[1], (D,), jnp.float32), 0.5, 1.5).astype(jnp.bfloat16)
    w_query = scatter_about(arg_keys[2], (D, HD), (D * 16) ** -0.5, 0.03125, ((0, 8), (1, 2)))
    w_key = scatter_about(arg_keys[3], (D, HD), D ** -0.5, 0.125, ((0, 8), (1, 2)))
    w_value = scatter_about(arg_keys[4], (D, HD), D ** -0.5, 0.125, ((0, 8), (1, 2)))
    w_out = scatter_about(arg_keys[5], (D, HD), (HD // 4) ** -0.5, 0.25, ((0, 8), (1, 2)))
    bias_table = scatter_about(arg_keys[6], (BUCKETS, H), 0.5, 3.0, ((1, 2),))
    buckets = set_ends(jax.random.randint(arg_keys[7], (2 * LEN - 1,), 0, BUCKETS), jax.random.fold_in(arg_keys[7], 1), 0, BUCKETS - 1).astype(jnp.int32)
    gain_ffn = jnp.clip(1.0 + 0.1 * jax.random.normal(arg_keys[8], (D,), jnp.float32), 0.5, 1.5).astype(jnp.bfloat16)
    w_gate = scatter_about(arg_keys[9], (D, FF), D ** -0.5, 0.125, ((0, 8), (1, 2)))
    w_up = scatter_about(arg_keys[10], (D, FF), D ** -0.5, 0.125, ((0, 8), (1, 2)))
    w_down = scatter_about(arg_keys[11], (D, FF), FF ** -0.5, 0.078125, ((0, 8), (1, 2)))
    cotangent = noise_with(arg_keys[12], (SEQS, LEN, D), 1.0, 6.0, ((0, 8), (1, 2)), (0, 2, 8, 2.0))
    return dict(inputs=inputs, gain_attn=gain_attn, w_query=w_query, w_key=w_key, w_value=w_value, w_out=w_out, bias_table=bias_table, buckets=buckets, gain_ffn=gain_ffn, w_gate=w_gate, w_up=w_up, w_down=w_down, cotangent=cotangent)


EPS = 1e-06

@jax.custom_vjp
def low(v):
    return lax.optimization_barrier(v.astype(jnp.bfloat16)).astype(jnp.float32)

@jax.custom_vjp
def low_back(v):
    return v

def low_keep(v):
    return (low(v), None)

def low_pass(kept, grad):
    return (grad,)

def back_keep(v):
    return (v, None)

def back_low(kept, grad):
    return (low(grad),)
low.defvjp(low_keep, low_pass)
low_back.defvjp(back_keep, back_low)

def matmul(left, right):
    return jnp.dot(left, right, precision=lax.Precision.HIGHEST, preferred_element_type=jnp.float32)

def gelu_tanh(value):
    return 0.5 * value * (1.0 + jnp.tanh(0.7978845608028654 * (value + 0.044715 * value * value * value)))

def rms_scale(value, gain):
    return value * lax.rsqrt(lax.optimization_barrier(jnp.mean(value * value, axis=-1, keepdims=True)) + EPS) * gain

def forward(inputs, gain_attn, w_query, w_key, w_value, w_out, bias_table, gain_ffn, w_gate, w_up, w_down, buckets):
    rows_in = inputs.reshape(SEQS * LEN, D)
    normed_attn = low(rms_scale(rows_in, gain_attn))
    queries = low_back(low(matmul(normed_attn, w_query))).reshape(SEQS, LEN, H, DH)
    keys = low_back(low(matmul(normed_attn, w_key))).reshape(SEQS, LEN, H, DH)
    values = low_back(low(matmul(normed_attn, w_value))).reshape(SEQS, LEN, H, DH)
    positions = jnp.arange(LEN, dtype=jnp.int32)
    offsets = positions[None, :] - positions[:, None] + (LEN - 1)
    bias_full = jnp.transpose(bias_table[buckets[offsets]], (2, 0, 1))

    def attend_one(blocks_in):
        query_seq, key_seq, value_seq = blocks_in
        scores = low_back(jnp.einsum('qhd,khd->hqk', query_seq, key_seq, precision=lax.Precision.HIGHEST)) + bias_full
        row_top = lax.optimization_barrier(jnp.max(scores, axis=-1, keepdims=True))
        raw_weight = jnp.exp(scores - row_top)
        probs_full = raw_weight / lax.optimization_barrier(jnp.sum(raw_weight, axis=-1, keepdims=True))
        return jnp.einsum('hqk,khd->qhd', low(probs_full), value_seq, precision=lax.Precision.HIGHEST)
    attended = lax.map(jax.checkpoint(attend_one), (queries, keys, values))
    attended = low_back(low(attended.reshape(SEQS * LEN, HD)))
    hidden = rows_in + low_back(matmul(attended, w_out.T))
    normed_ffn = low(rms_scale(hidden, gain_ffn))
    gate_pre = low_back(matmul(normed_ffn, w_gate))
    up_pre = low_back(matmul(normed_ffn, w_up))
    activ = low(gelu_tanh(gate_pre) * up_pre)
    output = hidden + low_back(matmul(activ, w_down.T))
    return output.reshape(SEQS, LEN, D)

def reference(inputs, gain_attn, w_query, w_key, w_value, w_out, bias_table, buckets, gain_ffn, w_gate, w_up, w_down, cotangent):
    output, pullback = jax.vjp(partial(forward, buckets=buckets), inputs.astype(jnp.float32), gain_attn.astype(jnp.float32), w_query.astype(jnp.float32), w_key.astype(jnp.float32), w_value.astype(jnp.float32), w_out.astype(jnp.float32), bias_table.astype(jnp.float32), gain_ffn.astype(jnp.float32), w_gate.astype(jnp.float32), w_up.astype(jnp.float32), w_down.astype(jnp.float32))
    grads = pullback(cotangent.astype(jnp.float32))
    return (output.astype(jnp.bfloat16), grads[0].astype(jnp.bfloat16), grads[1], grads[2], grads[3], grads[4], grads[5], grads[6], grads[7], grads[8], grads[9], grads[10])
```

```python
import functools

import jax
import jax.numpy as jnp
from jax import lax
from jax.experimental import pallas as pl
from jax.experimental.pallas import tpu as pltpu
from jax.sharding import PartitionSpec as P


DH = 64
EPS = 1e-06
LANES = 128
BF = jnp.bfloat16
F32 = jnp.float32
NT = (((1,), (1,)), ((), ()))
NN = (((1,), (0,)), ((), ()))
TN = (((0,), (0,)), ((), ()))


def dot(left, right, dims=NN, out=F32):
    return lax.dot_general(left, right, dims, preferred_element_type=F32).astype(out)


def fill_toeplitz(row, table_ref, head):
    span = row.shape[1]
    base = jnp.broadcast_to(row, (8, span))
    block = pltpu.roll(base, span - 7, 1, stride=1, stride_axis=0)
    count = 8
    while count < LANES:
        block = jnp.concatenate([pltpu.roll(block, span - count, 1), block], axis=0)
        count *= 2
    table_ref[head] = block


def bias_start(pos_ref, query_block, key_row, block, length):
    key_block = key_row // block
    start = pos_ref[query_block] - pos_ref[key_block] - (key_row - key_block * block)
    return pl.multiple_of(start + length - LANES, LANES)


def raw_scores(pos_ref, keys, query, table_ref, head, tile, block, length):
    scores = dot(keys, query, NT)
    parts = []
    for row in range(0, length, LANES):
        start = bias_start(pos_ref, tile, row, block, length)
        parts.append(scores[row : row + LANES, :] + table_ref[head, :, pl.ds(start, block)])
    return parts


def column_max(parts):
    top = parts[0]
    for part in parts[1:]:
        top = jnp.maximum(top, part)
    return jnp.max(top, axis=0, keepdims=True)


def column_sum(parts):
    total = parts[0]
    for part in parts[1:]:
        total = total + part
    return jnp.sum(total, axis=0, keepdims=True)


def forward_kernel(
    pos_ref, qa, qb, ka, kb, va, vb, row_ref, out_a, out_b, table_ref, *, block, length
):
    keys = jnp.concatenate([ka[...], kb[...]], axis=0)
    values_t = jnp.concatenate([va[...], vb[...]], axis=0).T
    for head in range(2):
        fill_toeplitz(row_ref[0, head : head + 1, :], table_ref, head)
    low_lanes = lax.broadcasted_iota(jnp.int32, (block, LANES), 1) < DH
    half = qa.shape[0] // block
    for tile in range(2 * half):
        source, target = (qa, out_a) if tile < half else (qb, out_b)
        spot = pl.ds((tile % half) * block, block)
        query = source[spot, :]
        mixed = []
        for head in range(2):
            mine = jnp.where(low_lanes == (head == 0), query, jnp.zeros_like(query))
            parts = raw_scores(pos_ref, keys, mine, table_ref, head, tile, block, length)
            top = column_max(parts)
            parts = [jnp.exp(part - top) for part in parts]
            scale = 1.0 / column_sum(parts)
            weight = jnp.concatenate([part.astype(BF) for part in parts], axis=0)
            mixed.append(dot(values_t[head * DH : (head + 1) * DH, :], weight) * scale)
        target[spot, :] = jnp.concatenate(mixed, axis=0).T.astype(BF)


def backward_kernel(
    pos_ref,
    qa,
    qb,
    ka,
    kb,
    va,
    vb,
    da,
    db,
    row_ref,
    grads_a,
    grads_b,
    diag_ref,
    table_ref,
    sums_ref,
    gk_ref,
    gv_ref,
    *,
    block,
    length,
):
    pair = pl.program_id(0)
    cols = grads_a.shape[1] // 3
    keys = jnp.concatenate([ka[...], kb[...]], axis=0)
    values = jnp.concatenate([va[...], vb[...]], axis=0)
    keys_t = keys.T
    for head in range(2):
        fill_toeplitz(row_ref[0, head : head + 1, :], table_ref, head)
    sums_ref[...] = jnp.zeros_like(sums_ref)
    low_lanes = lax.broadcasted_iota(jnp.int32, (block, LANES), 1) < DH
    half = qa.shape[0] // block

    def place(start):
        return pl.ds(pl.multiple_of(start + pair * LANES, LANES), LANES)

    for tile in range(2 * half):
        query_ref, grad_ref, target = (qa, da, grads_a) if tile < half else (qb, db, grads_b)
        spot = pl.ds((tile % half) * block, block)
        query, grad = query_ref[spot, :], grad_ref[spot, :]
        mixed, key_part, value_part = [], None, None
        for head in range(2):
            pick = low_lanes == (head == 0)
            mine = jnp.where(pick, query, jnp.zeros_like(query))
            back = jnp.where(pick, grad, jnp.zeros_like(grad))
            parts = raw_scores(pos_ref, keys, mine, table_ref, head, tile, block, length)
            top = column_max(parts)
            parts = [jnp.exp(part - top) for part in parts]
            scale = 1.0 / column_sum(parts)
            parts = [part * scale for part in parts]
            probs_low = jnp.concatenate([part.astype(BF) for part in parts], axis=0)
            grad_probs = dot(values, back, NT)
            moved = [
                part * grad_probs[row * LANES : (row + 1) * LANES, :]
                for row, part in enumerate(parts)
            ]
            delta = column_sum(moved)
            moved = [both - part * delta for both, part in zip(moved, parts)]
            for row, part in enumerate(moved):
                start = bias_start(pos_ref, tile, row * LANES, block, length)
                where = (head, slice(None), pl.ds(start, block))
                sums_ref[where] = sums_ref[where] + part
            scores_low = jnp.concatenate([part.astype(BF) for part in moved], axis=0)
            mixed.append(dot(keys_t[head * DH : (head + 1) * DH, :], scores_low))
            gv, gk = dot(probs_low, back), dot(scores_low, mine)
            value_part = gv if value_part is None else value_part + gv
            key_part = gk if key_part is None else key_part + gk
        target[spot, place(0)] = jnp.concatenate(mixed, axis=0).T.astype(BF)
        if tile:
            gk_ref[...] += key_part
            gv_ref[...] += value_part
        else:
            gk_ref[...] = key_part
            gv_ref[...] = value_part
    rows = qa.shape[0]
    grads_a[:, place(cols)] = gk_ref[:rows, :].astype(BF)
    grads_b[:, place(cols)] = gk_ref[rows:, :].astype(BF)
    grads_a[:, place(2 * cols)] = gv_ref[:rows, :].astype(BF)
    grads_b[:, place(2 * cols)] = gv_ref[rows:, :].astype(BF)
    for head in range(2):
        folded = sums_ref[head]
        count = LANES // 2
        while count >= 8:
            folded = pltpu.roll(folded[:count], count, 1) + folded[count:]
            count //= 2
        diag_ref[0, head] = folded


def attention_specs(rows, pairs, span, block):
    def column(offset):
        return pl.BlockSpec((rows, LANES), lambda p, pos, o=offset: (0, o * pairs + p))

    specs = [column(part) for part in (0, 0, 1, 1, 2, 2)]
    row = pl.BlockSpec((1, 2, span), lambda p, pos: (p, 0, 0))
    return column, specs, row


def attention_forward(own, other, rows_rev, pos, block):
    rows, width = own.shape
    cols, length = width // 3, 2 * rows
    pairs, span = cols // LANES, rows_rev.shape[2]
    column, specs, row = attention_specs(rows, pairs, span, block)
    shape = jax.ShapeDtypeStruct((rows, cols), BF)
    return pl.pallas_call(
        functools.partial(forward_kernel, block=block, length=length),
        out_shape=(shape, shape),
        grid_spec=pltpu.PrefetchScalarGridSpec(
            num_scalar_prefetch=1,
            grid=(pairs,),
            in_specs=specs + [row],
            out_specs=(column(0), column(0)),
            scratch_shapes=[pltpu.VMEM((2, LANES, span), F32)],
        ),
        compiler_params=pltpu.CompilerParams(vmem_limit_bytes=40 << 20),
        cost_estimate=pl.CostEstimate(
            flops=16 * length * length * cols,
            bytes_accessed=16 * length * cols,
            transcendentals=length * length * cols // DH,
        ),
        name="attend",
    )(pos, own, other, own, other, own, other, rows_rev)


def attention_backward(own, other, grad_own, grad_other, rows_rev, pos, block):
    rows, width = own.shape
    cols, length = width // 3, 2 * rows
    pairs, span = cols // LANES, rows_rev.shape[2]
    column, specs, row = attention_specs(rows, pairs, span, block)
    shape = jax.ShapeDtypeStruct((rows, width), BF)
    whole = pl.BlockSpec((rows, width), lambda p, pos: (0, 0))
    return pl.pallas_call(
        functools.partial(backward_kernel, block=block, length=length),
        out_shape=(shape, shape, jax.ShapeDtypeStruct((pairs, 2, 8, span), F32)),
        grid_spec=pltpu.PrefetchScalarGridSpec(
            num_scalar_prefetch=1,
            grid=(pairs,),
            in_specs=specs + [column(0), column(0), row],
            out_specs=(
                whole,
                whole,
                pl.BlockSpec((1, 2, 8, span), lambda p, pos: (p, 0, 0, 0)),
            ),
            scratch_shapes=[
                pltpu.VMEM((2, LANES, span), F32),
                pltpu.VMEM((2, LANES, span), F32),
                pltpu.VMEM((length, LANES), F32),
                pltpu.VMEM((length, LANES), F32),
            ],
        ),
        compiler_params=pltpu.CompilerParams(vmem_limit_bytes=48 << 20),
        cost_estimate=pl.CostEstimate(
            flops=40 * length * length * cols,
            bytes_accessed=32 * length * cols,
            transcendentals=length * length * cols // DH,
        ),
        name="attend_back",
    )(pos, own, other, own, other, own, other, grad_own, grad_other, rows_rev)


def enter_kernel(info_ref, in_ref, cot_ref, kept_ref, normed_ref, grad_ref):
    blocks = info_ref.shape[0] - 1
    step = in_ref.shape[1] // blocks
    value = in_ref[...].astype(F32)
    scale = lax.rsqrt(jnp.mean(value * value, axis=-1, keepdims=True) + EPS)
    for index in range(blocks):
        source = pl.ds(pl.multiple_of(info_ref[index + 1] * step, step), step)
        target = pl.ds(index * step, step)
        piece = in_ref[:, source]
        kept_ref[:, target] = piece
        normed_ref[:, target] = (piece.astype(F32) * scale).astype(BF)
        grad_ref[:, target] = cot_ref[:, source]


def enter(info, inputs, cotangent):
    rows, width = inputs.shape
    spec_in = pl.BlockSpec((rows // 2, width), lambda r, info: (jnp.bitwise_xor(r, info[0]), 0))
    spec_out = pl.BlockSpec((rows // 2, width), lambda r, info: (r, 0))
    shape = jax.ShapeDtypeStruct((rows, width), BF)
    return pl.pallas_call(
        enter_kernel,
        out_shape=(shape, shape, shape),
        grid_spec=pltpu.PrefetchScalarGridSpec(
            num_scalar_prefetch=1,
            grid=(2,),
            in_specs=[spec_in, spec_in],
            out_specs=(spec_out,) * 3,
        ),
        name="enter",
    )(info, inputs, cotangent)


def leave_kernel(info_ref, mine_ref, other_ref, out_ref):
    blocks = info_ref.shape[0] - 1
    rows = mine_ref.shape[0]
    step = mine_ref.shape[1] // blocks
    first = pl.ds(pl.multiple_of(info_ref[0] * rows, rows), rows)
    second = pl.ds(pl.multiple_of((1 - info_ref[0]) * rows, rows), rows)
    for index in range(blocks):
        target = pl.ds(pl.multiple_of(info_ref[index + 1] * step, step), step)
        source = pl.ds(index * step, step)
        out_ref[first, target] = mine_ref[:, source]
        out_ref[second, target] = other_ref[:, source]


def leave(info, mine, other):
    rows, width = mine.shape
    spec = pl.BlockSpec((rows, width), lambda r, info: (0, 0))
    return pl.pallas_call(
        leave_kernel,
        out_shape=jax.ShapeDtypeStruct((2 * rows, width), BF),
        grid_spec=pltpu.PrefetchScalarGridSpec(
            num_scalar_prefetch=1,
            grid=(1,),
            in_specs=[spec, spec],
            out_specs=pl.BlockSpec((2 * rows, width), lambda r, info: (0, 0)),
        ),
        name="leave",
    )(info, mine, other)


class Plane:
    def __init__(self, count):
        self.inner = 2
        self.outer = count // self.inner
        self.count = count
        self.direct = count in (4, 8)

    def order(self):
        if not self.direct:
            return [0]
        me = lax.axis_index("fsdp")
        line, side = me // self.inner, me % self.inner
        found = []
        for flip in range(self.inner):
            for step in range(self.outer):
                place = (line - step + self.outer) % self.outer
                found.append(place * self.inner + (side + flip) % self.inner)
        return found

    def along(self, value, step):
        pairs = []
        for index in range(self.count):
            line, side = index // self.inner, index % self.inner
            pairs.append((index, (line + step) % self.outer * self.inner + side))
        return lax.ppermute(value, "fsdp", pairs)

    def across(self, value):
        pairs = [
            (index, index // self.inner * self.inner + (index + 1) % self.inner)
            for index in range(self.count)
        ]
        return lax.ppermute(value, "fsdp", pairs)

    def gather(self, shard):
        if not self.direct:
            return lax.all_gather(shard, "fsdp", axis=0, tiled=True)
        pieces = [shard] + [self.along(shard, step) for step in range(1, self.outer)]
        pieces = pieces + [self.across(piece) for piece in pieces]
        return jnp.concatenate(pieces, axis=0)

    def add_up(self, value):
        if not self.direct:
            return lax.psum(value, "fsdp")
        value = value + self.across(value)
        return value + sum(self.along(value, step) for step in range(1, self.outer))

    def scatter(self, whole):
        if not self.direct:
            return lax.psum_scatter(
                whole.astype(F32), "fsdp", scatter_dimension=0, tiled=True
            )
        rows = whole.shape[0] // self.inner
        came = self.across(whole[rows:])
        whole = (whole[:rows].astype(F32) + came.astype(F32)).astype(BF)
        step_rows = rows // self.outer
        total = whole[:step_rows].astype(F32)
        for step in range(1, self.outer):
            piece = whole[step * step_rows : (step + 1) * step_rows]
            total = total + self.along(piece, -step).astype(F32)
        return total


def swap(value, axis):
    return lax.ppermute(value, axis, [(0, 1), (1, 0)])


def share(mine):
    partner = swap(mine, "tp")
    return jnp.concatenate([mine, partner], axis=0), share_other(mine)


def share_other(mine):
    far = swap(mine, "ctx")
    return jnp.concatenate([far, swap(far, "tp")], axis=0)


def reduce_other(partial):
    rows = partial.shape[0] // 2
    came = swap(partial[rows:], "tp")
    chip = (partial[:rows].astype(F32) + came.astype(F32)).astype(BF)
    return swap(chip, "ctx")


def reduce_own(partial, far):
    rows = partial.shape[0] // 2
    came = swap(partial[rows:], "tp")
    return partial[:rows].astype(F32) + came.astype(F32) + far.astype(F32)


def gelu_parts(value):
    inner = 0.7978845608028654 * (value + 0.044715 * value * value * value)
    tanh = jnp.tanh(inner)
    slope = 0.7978845608028654 * (1.0 + 3.0 * 0.044715 * value * value)
    gelu = 0.5 * value * (1.0 + tanh)
    back = 0.5 * (1.0 + tanh) + 0.5 * value * (1.0 - tanh * tanh) * slope
    return gelu, back


def tied(value, *deps):
    return lax.optimization_barrier((value,) + deps)[0]


def shards(
    plane,
    inputs,
    gain_attn,
    w_query,
    w_key,
    w_value,
    w_out,
    bias_table,
    buckets,
    gain_ffn,
    w_gate,
    w_up,
    w_down,
    cotangent,
):
    seq_dev, tokens, width = inputs.shape
    block = tokens // 2
    length = 2 * tokens
    ctx, tp = lax.axis_index("ctx"), lax.axis_index("tp")
    own_rows = w_query.shape[0]
    head_cols, ffn_cols = w_query.shape[1] // 2, w_gate.shape[1] // 2
    heads = bias_table.shape[1] // 2

    def mine(weight):
        count = weight.shape[1] // 2
        return lax.dynamic_slice_in_dim(weight, ctx * count, count, axis=1)

    def scaled(weight, gain):
        return (mine(weight).astype(F32) * gain.astype(F32)[:, None]).astype(BF)

    order = plane.order()
    info = jnp.stack([tp] + order).astype(jnp.int32)
    pos = jnp.stack(
        [
            ((ctx + far) % 2) * tokens + ((tp + turn) % 2) * block
            for far in range(2)
            for turn in range(2)
        ]
    ).astype(jnp.int32)

    qkv_shard = jnp.concatenate(
        [scaled(weight, gain_attn) for weight in (w_query, w_key, w_value)], axis=1
    )
    ffn_shard = jnp.concatenate([scaled(w_gate, gain_ffn), scaled(w_up, gain_ffn)], axis=1)
    qkv_full = plane.gather(qkv_shard)
    kept, normed, grad_own = enter(info, inputs[0], cotangent[0])
    kept, grad_mine = kept[:block].astype(F32), grad_own[:block]
    normed_other = share_other(normed[:block])
    grad_other = share_other(grad_mine)
    out_full = plane.gather(mine(w_out))
    ffn_full = plane.gather(ffn_shard)
    down_full = plane.gather(mine(w_down))

    table = lax.dynamic_slice_in_dim(bias_table, ctx * heads, heads, axis=1)
    reach = 2 * length
    reversed_buckets = jnp.pad(buckets[::-1], (0, 1), constant_values=-1)
    hits = (
        jnp.arange(bias_table.shape[0], dtype=jnp.int32)[:, None] == reversed_buckets[None, :]
    ).astype(F32)
    rows_rev = lax.dot_general(
        table.astype(F32),
        hits,
        TN,
        precision=lax.Precision.HIGHEST,
        preferred_element_type=F32,
    ).reshape(heads // 2, 2, reach)

    qkv_own = dot(normed, qkv_full, NN, BF)
    qkv_other = dot(normed_other, qkv_full, NN, BF)
    att_own, att_other = attention_forward(qkv_own, qkv_other, rows_rev, pos, block)
    far = reduce_other(dot(att_other, out_full, NT, BF))
    hidden = kept + reduce_own(dot(att_own, out_full, NT, BF), far)

    rms_two = lax.rsqrt(jnp.mean(hidden * hidden, axis=-1, keepdims=True) + EPS)
    normed_two = (hidden * rms_two).astype(BF)
    two_own, two_other = share(normed_two)

    def ffn(normed_rows, grad_rows):
        pre = dot(normed_rows, ffn_full)
        gate, up = pre[:, :ffn_cols], pre[:, ffn_cols:]
        gelu, back = gelu_parts(gate)
        activ = (gelu * up).astype(BF)
        grad_activ = dot(grad_rows, down_full)
        both = jnp.concatenate(
            [(back * up * grad_activ).astype(BF), (gelu * grad_activ).astype(BF)], axis=1
        )
        return activ, both

    act_own, both_own = ffn(two_own, grad_own)
    act_other, both_other = ffn(two_other, grad_other)

    far = reduce_other(dot(both_other, ffn_full, NT, BF))
    back_two = reduce_own(dot(both_own, ffn_full, NT, BF), far)
    grad_hidden = (
        grad_mine.astype(F32)
        + rms_two * back_two
        - hidden * rms_two**3 * jnp.mean(hidden * back_two, axis=-1, keepdims=True)
    )
    branch_own, branch_other = share(grad_hidden.astype(BF))

    far = reduce_other(dot(act_other, down_full, NT, BF))
    result = (hidden + reduce_own(dot(act_own, down_full, NT, BF), far)).astype(BF)
    result = leave(info, result, swap(result, "tp"))

    gatt_own = dot(branch_own, out_full, NN, BF)
    gatt_other = dot(branch_other, out_full, NN, BF)
    gqkv_own, gqkv_other, diag = attention_backward(
        qkv_own, qkv_other, gatt_own, gatt_other, rows_rev, pos, block
    )
    far = reduce_other(dot(gqkv_other, qkv_full, NT, BF))
    back_one = reduce_own(dot(gqkv_own, qkv_full, NT, BF), far)
    rms_one = lax.rsqrt(jnp.mean(kept * kept, axis=-1, keepdims=True) + EPS)
    input_grad = (
        grad_hidden
        + rms_one * back_one
        - kept * rms_one**3 * jnp.mean(kept * back_one, axis=-1, keepdims=True)
    ).astype(BF)
    input_grad = leave(info, input_grad, swap(input_grad, "tp"))

    def outer(left_own, left_other, right_own, right_other):
        return dot(
            jnp.concatenate([left_own, left_other], axis=0),
            jnp.concatenate([right_own, right_other], axis=0),
            TN,
            BF,
        )

    half_rows = own_rows // 2

    def settle(total, parts):
        keep = lax.dynamic_slice_in_dim(total, ctx * half_rows, half_rows)
        give = lax.dynamic_slice_in_dim(total, (1 - ctx) * half_rows, half_rows)
        came = swap(give.astype(BF), "ctx").astype(F32)
        found = []
        count = total.shape[1] // parts
        for part in range(parts):
            here = keep[:, part * count : (part + 1) * count]
            there = came[:, part * count : (part + 1) * count]
            found.append(
                jnp.where(
                    ctx == 0,
                    jnp.concatenate([here, there], axis=1),
                    jnp.concatenate([there, here], axis=1),
                )
            )
        return found

    def own_half(weight):
        return lax.dynamic_slice_in_dim(weight, ctx * half_rows, half_rows).astype(F32)

    def gain_grad(grads, weights):
        total = sum(jnp.sum(grad * own_half(weight), axis=1) for grad, weight in zip(grads, weights))
        return total + swap(total, "tp")

    (down_grad,) = settle(plane.scatter(outer(grad_own, grad_other, act_own, act_other)), 1)
    ffn_grads = settle(plane.scatter(outer(two_own, two_other, both_own, both_other)), 2)
    (out_grad,) = settle(plane.scatter(outer(branch_own, branch_other, att_own, att_other)), 1)
    qkv_grads = settle(plane.scatter(outer(normed, normed_other, gqkv_own, gqkv_other)), 3)
    gain_ffn_grad = gain_grad(ffn_grads, (w_gate, w_up))
    gain_attn_grad = gain_grad(qkv_grads, (w_query, w_key, w_value))
    scale_one, scale_two = own_half(gain_attn)[:, None], own_half(gain_ffn)[:, None]
    qkv_grads = [scale_one * grad for grad in qkv_grads]
    ffn_grads = [scale_two * grad for grad in ffn_grads]

    diag = diag.reshape(heads, 8, reach)
    shifted = sum(jnp.roll(diag[:, row, :], 7 - row, axis=1) for row in range(8))
    table_part = lax.dot_general(
        hits, shifted, NT, precision=lax.Precision.HIGHEST, preferred_element_type=F32
    )
    table_part = plane.add_up(table_part)
    table_far = swap(table_part, "ctx")
    table_grad = jnp.where(
        ctx == 0,
        jnp.concatenate([table_part, table_far], axis=1),
        jnp.concatenate([table_far, table_part], axis=1),
    )

    return (
        result[None],
        input_grad[None],
        gain_attn_grad,
        *qkv_grads,
        out_grad,
        table_grad,
        gain_ffn_grad,
        *ffn_grads,
        down_grad,
    )


def solution(mesh):
    plane = Plane(mesh.shape["fsdp"])
    placed = (
        P("fsdp", "ctx", None),
        P("fsdp"),
        P("fsdp", "tp"),
        P("fsdp", "tp"),
        P("fsdp", "tp"),
        P("fsdp", "tp"),
        P(None, "tp"),
        P(),
        P("fsdp"),
        P("fsdp", "tp"),
        P("fsdp", "tp"),
        P("fsdp", "tp"),
        P("fsdp", "ctx", None),
    )
    rows = P(("fsdp", "ctx"))
    matrix = P(("fsdp", "ctx"), "tp")
    return jax.shard_map(
        functools.partial(shards, plane),
        mesh=mesh,
        in_specs=placed,
        out_specs=(
            P("fsdp", "ctx", None),
            P("fsdp", "ctx", None),
            rows,
            matrix,
            matrix,
            matrix,
            matrix,
            P(None, "tp"),
            rows,
            matrix,
            matrix,
            matrix,
        ),
        check_vma=False,
    )
```

```python
import functools

import jax
import jax.numpy as jnp
from jax import lax
from jax.experimental import pallas as pl
from jax.experimental.pallas import tpu as pltpu
from jax.sharding import PartitionSpec as P


DH = 64
EPS = 1e-06
LANES = 128
BF = jnp.bfloat16
F32 = jnp.float32
NT = (((1,), (1,)), ((), ()))
NN = (((1,), (0,)), ((), ()))
TN = (((0,), (0,)), ((), ()))


def dot(left, right, dims=NN, out=F32):
    return lax.dot_general(left, right, dims, preferred_element_type=F32).astype(out)


def fill_toeplitz(row, table_ref, head):
    span = row.shape[1]
    base = jnp.broadcast_to(row, (8, span))
    block = pltpu.roll(base, span - 7, 1, stride=1, stride_axis=0)
    count = 8
    while count < LANES:
        block = jnp.concatenate([pltpu.roll(block, span - count, 1), block], axis=0)
        count *= 2
    table_ref[head] = block


def bias_start(pos_ref, query_block, key_row, block, length):
    key_block = key_row // block
    start = pos_ref[query_block] - pos_ref[key_block] - (key_row - key_block * block)
    return pl.multiple_of(start + length - LANES, LANES)


def raw_scores(pos_ref, keys, query, table_ref, head, tile, block, length):
    scores = dot(keys, query, NT)
    parts = []
    for row in range(0, length, LANES):
        start = bias_start(pos_ref, tile, row, block, length)
        parts.append(scores[row : row + LANES, :] + table_ref[head, :, pl.ds(start, block)])
    return parts


def column_max(parts):
    top = parts[0]
    for part in parts[1:]:
        top = jnp.maximum(top, part)
    return jnp.max(top, axis=0, keepdims=True)


def column_sum(parts):
    total = parts[0]
    for part in parts[1:]:
        total = total + part
    return jnp.sum(total, axis=0, keepdims=True)


def forward_kernel(pos_ref, q_ref, k_ref, v_ref, row_ref, out_ref, table_ref, *, block):
    length = q_ref.shape[0]

    @pl.when(pl.program_id(1) == 0)
    def _():
        for head in range(2):
            fill_toeplitz(row_ref[0, head : head + 1, :], table_ref, head)

    keys = k_ref[...]
    values_t = v_ref[...].T
    low_lanes = lax.broadcasted_iota(jnp.int32, (block, LANES), 1) < DH
    for tile in range(length // block):
        spot = pl.ds(tile * block, block)
        query = q_ref[spot, :]
        mixed = []
        for head in range(2):
            mine = jnp.where(low_lanes == (head == 0), query, jnp.zeros_like(query))
            parts = raw_scores(pos_ref, keys, mine, table_ref, head, tile, block, length)
            top = column_max(parts)
            parts = [jnp.exp(part - top) for part in parts]
            scale = 1.0 / column_sum(parts)
            weight = jnp.concatenate([part.astype(BF) for part in parts], axis=0)
            mixed.append(dot(values_t[head * DH : (head + 1) * DH, :], weight) * scale)
        out_ref[spot, :] = jnp.concatenate(mixed, axis=0).T.astype(BF)


def backward_kernel(
    pos_ref,
    q_ref,
    k_ref,
    v_ref,
    d_ref,
    row_ref,
    grads_ref,
    diag_ref,
    table_ref,
    sums_ref,
    gk_ref,
    gv_ref,
    *,
    block,
):
    pair, seq = pl.program_id(0), pl.program_id(1)
    length = q_ref.shape[0]
    cols = grads_ref.shape[1] // 3

    @pl.when(seq == 0)
    def _():
        for head in range(2):
            fill_toeplitz(row_ref[0, head : head + 1, :], table_ref, head)
        sums_ref[...] = jnp.zeros_like(sums_ref)

    keys, values = k_ref[...], v_ref[...]
    keys_t = keys.T
    low_lanes = lax.broadcasted_iota(jnp.int32, (block, LANES), 1) < DH

    def place(start):
        return pl.ds(pl.multiple_of(start + pair * LANES, LANES), LANES)

    for tile in range(length // block):
        spot = pl.ds(tile * block, block)
        query, grad = q_ref[spot, :], d_ref[spot, :]
        mixed, key_part, value_part = [], None, None
        for head in range(2):
            pick = low_lanes == (head == 0)
            mine = jnp.where(pick, query, jnp.zeros_like(query))
            back = jnp.where(pick, grad, jnp.zeros_like(grad))
            parts = raw_scores(pos_ref, keys, mine, table_ref, head, tile, block, length)
            top = column_max(parts)
            parts = [jnp.exp(part - top) for part in parts]
            scale = 1.0 / column_sum(parts)
            parts = [part * scale for part in parts]
            probs_low = jnp.concatenate([part.astype(BF) for part in parts], axis=0)
            grad_probs = dot(values, back, NT)
            moved = [
                part * grad_probs[row * LANES : (row + 1) * LANES, :]
                for row, part in enumerate(parts)
            ]
            delta = column_sum(moved)
            moved = [both - part * delta for both, part in zip(moved, parts)]
            for row, part in enumerate(moved):
                start = bias_start(pos_ref, tile, row * LANES, block, length)
                where = (head, slice(None), pl.ds(start, block))
                sums_ref[where] = sums_ref[where] + part
            scores_low = jnp.concatenate([part.astype(BF) for part in moved], axis=0)
            mixed.append(dot(keys_t[head * DH : (head + 1) * DH, :], scores_low))
            gv, gk = dot(probs_low, back), dot(scores_low, mine)
            value_part = gv if value_part is None else value_part + gv
            key_part = gk if key_part is None else key_part + gk
        rows = pl.ds(pl.multiple_of(seq * length + tile * block, block), block)
        grads_ref[rows, place(0)] = jnp.concatenate(mixed, axis=0).T.astype(BF)
        if tile:
            gk_ref[...] += key_part
            gv_ref[...] += value_part
        else:
            gk_ref[...] = key_part
            gv_ref[...] = value_part
    rows = pl.ds(pl.multiple_of(seq * length, length), length)
    grads_ref[rows, place(cols)] = gk_ref[...].astype(BF)
    grads_ref[rows, place(2 * cols)] = gv_ref[...].astype(BF)

    @pl.when(seq == pl.num_programs(1) - 1)
    def _():
        for head in range(2):
            folded = sums_ref[head]
            count = LANES // 2
            while count >= 8:
                folded = pltpu.roll(folded[:count], count, 1) + folded[count:]
                count //= 2
            diag_ref[0, head] = folded


def attention_specs(length, pairs, span):
    def column(offset):
        return pl.BlockSpec((length, LANES), lambda p, e, pos, o=offset: (e, o * pairs + p))

    row = pl.BlockSpec((1, 2, span), lambda p, e, pos: (p, 0, 0))
    return column, [column(part) for part in range(3)], row


def attention_forward(qkv, rows_rev, pos, block, length):
    rows, width = qkv.shape
    cols = width // 3
    pairs, span = cols // LANES, rows_rev.shape[2]
    column, specs, row = attention_specs(length, pairs, span)
    return pl.pallas_call(
        functools.partial(forward_kernel, block=block),
        out_shape=jax.ShapeDtypeStruct((rows, cols), BF),
        grid_spec=pltpu.PrefetchScalarGridSpec(
            num_scalar_prefetch=1,
            grid=(pairs, rows // length),
            in_specs=specs + [row],
            out_specs=column(0),
            scratch_shapes=[pltpu.VMEM((2, LANES, span), F32)],
        ),
        compiler_params=pltpu.CompilerParams(vmem_limit_bytes=40 << 20),
        cost_estimate=pl.CostEstimate(
            flops=16 * length * rows * cols,
            bytes_accessed=8 * rows * cols,
            transcendentals=length * rows * cols // DH,
        ),
        name="attend",
    )(pos, qkv, qkv, qkv, rows_rev)


def attention_backward(qkv, grad, rows_rev, pos, block, length):
    rows, width = qkv.shape
    cols = width // 3
    pairs, span = cols // LANES, rows_rev.shape[2]
    column, specs, row = attention_specs(length, pairs, span)
    return pl.pallas_call(
        functools.partial(backward_kernel, block=block),
        out_shape=(
            jax.ShapeDtypeStruct((rows, width), BF),
            jax.ShapeDtypeStruct((pairs, 2, 8, span), F32),
        ),
        grid_spec=pltpu.PrefetchScalarGridSpec(
            num_scalar_prefetch=1,
            grid=(pairs, rows // length),
            in_specs=specs + [column(0), row],
            out_specs=(
                pl.BlockSpec((rows, width), lambda p, e, pos: (0, 0)),
                pl.BlockSpec((1, 2, 8, span), lambda p, e, pos: (p, 0, 0, 0)),
            ),
            scratch_shapes=[
                pltpu.VMEM((2, LANES, span), F32),
                pltpu.VMEM((2, LANES, span), F32),
                pltpu.VMEM((length, LANES), F32),
                pltpu.VMEM((length, LANES), F32),
            ],
        ),
        compiler_params=pltpu.CompilerParams(vmem_limit_bytes=48 << 20),
        cost_estimate=pl.CostEstimate(
            flops=40 * length * rows * cols,
            bytes_accessed=16 * rows * cols,
            transcendentals=length * rows * cols // DH,
        ),
        name="attend_back",
    )(pos, qkv, qkv, qkv, grad, rows_rev)


def enter_kernel(info_ref, in_ref, cot_ref, kept_ref, normed_ref, grad_ref):
    blocks = info_ref.shape[0] - 1
    step = in_ref.shape[1] // blocks
    value = in_ref[...].astype(F32)
    scale = lax.rsqrt(jnp.mean(value * value, axis=-1, keepdims=True) + EPS)
    for index in range(blocks):
        source = pl.ds(pl.multiple_of(info_ref[index + 1] * step, step), step)
        target = pl.ds(index * step, step)
        piece = in_ref[:, source]
        kept_ref[:, target] = piece
        normed_ref[:, target] = (piece.astype(F32) * scale).astype(BF)
        grad_ref[:, target] = cot_ref[:, source]


def enter(info, inputs, cotangent):
    rows, width = inputs.shape
    spec_in = pl.BlockSpec((rows // 2, width), lambda r, info: (jnp.bitwise_xor(r, info[0]), 0))
    spec_out = pl.BlockSpec((rows // 2, width), lambda r, info: (r, 0))
    shape = jax.ShapeDtypeStruct((rows, width), BF)
    return pl.pallas_call(
        enter_kernel,
        out_shape=(shape, shape, shape),
        grid_spec=pltpu.PrefetchScalarGridSpec(
            num_scalar_prefetch=1,
            grid=(2,),
            in_specs=[spec_in, spec_in],
            out_specs=(spec_out,) * 3,
        ),
        name="enter",
    )(info, inputs, cotangent)


def leave_kernel(info_ref, mine_ref, other_ref, out_ref):
    blocks = info_ref.shape[0] - 1
    rows = mine_ref.shape[0]
    step = mine_ref.shape[1] // blocks
    first = pl.ds(pl.multiple_of(info_ref[0] * rows, rows), rows)
    second = pl.ds(pl.multiple_of((1 - info_ref[0]) * rows, rows), rows)
    for index in range(blocks):
        target = pl.ds(pl.multiple_of(info_ref[index + 1] * step, step), step)
        source = pl.ds(index * step, step)
        out_ref[first, target] = mine_ref[:, source]
        out_ref[second, target] = other_ref[:, source]


def leave(info, mine, other):
    rows, width = mine.shape
    spec = pl.BlockSpec((rows, width), lambda r, info: (0, 0))
    return pl.pallas_call(
        leave_kernel,
        out_shape=jax.ShapeDtypeStruct((2 * rows, width), BF),
        grid_spec=pltpu.PrefetchScalarGridSpec(
            num_scalar_prefetch=1,
            grid=(1,),
            in_specs=[spec, spec],
            out_specs=pl.BlockSpec((2 * rows, width), lambda r, info: (0, 0)),
        ),
        name="leave",
    )(info, mine, other)


def settle_kernel(info_ref, keep_ref, *refs, parts, scaled):
    moved, refs = refs[:3], refs[3:]
    weights, refs = (refs[:parts], refs[parts:]) if scaled else ((), refs)
    gain_ref, refs = (refs[0], refs[1:]) if scaled else (None, refs)
    outs = refs[:parts]
    cols = keep_ref.shape[1] // parts
    total = None
    for far in range(4):
        place = pl.multiple_of(jnp.bitwise_xor(info_ref[0], far) * cols, LANES)
        for part in range(parts):
            source = pl.ds(part * cols, cols)
            piece = keep_ref[:, source] if far == 0 else moved[far - 1][:, source].astype(F32)
            if scaled:
                weight = weights[part][:, pl.ds(place, cols)].astype(F32)
                along = jnp.sum(piece * weight, axis=1, keepdims=True)
                total = along if total is None else total + along
                piece = piece * gain_ref[...]
            outs[part][:, pl.ds(place, cols)] = piece
    if scaled:
        refs[parts][...] = jnp.broadcast_to(total, refs[parts].shape)


def settle(info, keep, moved, weights, gain, parts):
    rows, width = keep.shape
    cols = 4 * width // parts
    same = pl.BlockSpec((rows, width), lambda i, info: (0, 0))
    half = pl.BlockSpec((rows, cols), lambda i, info: (jnp.bitwise_and(info[0], 1), 0))
    out_spec = pl.BlockSpec((rows, cols), lambda i, info: (0, 0))
    scaled = gain is not None
    operands = [keep, *moved]
    specs = [same] * 4
    out_specs = [out_spec] * parts
    shapes = [jax.ShapeDtypeStruct((rows, cols), F32)] * parts
    if scaled:
        operands += [*weights, gain]
        specs += [half] * parts
        specs += [pl.BlockSpec((rows, 1), lambda i, info: (jnp.bitwise_and(info[0], 1), 0))]
        out_specs += [pl.BlockSpec((rows, LANES), lambda i, info: (0, 0))]
        shapes += [jax.ShapeDtypeStruct((rows, LANES), F32)]
    return pl.pallas_call(
        functools.partial(settle_kernel, parts=parts, scaled=scaled),
        out_shape=shapes,
        grid_spec=pltpu.PrefetchScalarGridSpec(
            num_scalar_prefetch=1, grid=(1,), in_specs=specs, out_specs=out_specs
        ),
        name="settle",
    )(info, *operands)


class Plane:
    def __init__(self, count):
        self.count = count
        self.line = count // 2

    def permute(self, value, move):
        pairs = []
        for index in range(self.count):
            target = move(index // 2, index % 2)
            if target is not None:
                pairs.append((index, target[0] * 2 + target[1]))
        return lax.ppermute(value, "fsdp", pairs)

    def along(self, value, step):
        return self.permute(value, lambda z, y: ((z + step) % self.line, y))

    def hop(self, value, moves):
        return self.permute(value, lambda z, y: (moves[z], y) if z in moves else None)

    def across(self, value):
        return self.permute(value, lambda z, y: (z, 1 - y))

    def diagonal(self, value):
        pairs = []
        for index in range(self.count):
            for side in range(2):
                pairs.append((index * 2 + side, (index ^ 1) * 2 + 1 - side))
        return lax.ppermute(value, ("fsdp", "ctx"), pairs)

    def square(self, pieces):
        return [swap(pieces[1], "ctx"), self.across(pieces[2]), self.diagonal(pieces[3])]

    def recut(self, mine, theirs, side):
        came = self.across(theirs)
        return jnp.where(
            side == 0,
            jnp.concatenate([mine, came], axis=0),
            jnp.concatenate([came, mine], axis=0),
        )

    def ring(self, shard):
        pieces = [shard]
        for _ in range(self.line - 1):
            pieces.append(self.along(pieces[-1], 1))
        return pieces

    def pieces(self, shard, place, after):
        if self.line != 4:
            found = [shard] + [self.along(shard, step) for step in range(1, self.line)]
            return jnp.concatenate(found, axis=0)
        two = self.along(shard, 2)
        up = self.hop(shard, {0: 1, 1: 2, 2: 3})
        down = self.hop(shard, {1: 0, 2: 1, 3: 2})
        two, up, down, _ = lax.optimization_barrier((two, up, down, after))
        far = self.hop(two, {1: 0, 2: 3})
        found = [shard, jnp.where(place == 0, far, up), two, jnp.where(place == 3, far, down)]
        return jnp.concatenate(found, axis=0)

    def scatter(self, whole):
        rows = whole.shape[0] // self.line
        sent = [
            self.along(whole[step * rows : (step + 1) * rows], -step)
            for step in range(1, self.line)
        ]
        return whole[:rows], *sent

    def share(self, mine, partner=None):
        half = mine.shape[0] // 2
        partner = swap(mine, "tp") if partner is None else partner
        beside = swap(mine, "ctx")
        over = self.across(mine)
        corner = jnp.concatenate([swap(over[:half], "ctx"), self.across(beside[half:])], axis=0)
        return jnp.concatenate(
            [
                mine,
                partner,
                beside,
                swap(beside, "tp"),
                over,
                swap(over, "tp"),
                corner,
                swap(corner, "tp"),
            ],
            axis=0,
        )

    def chip_sums(self, beside, over, corner):
        rows = beside.shape[0] // 2
        chip = []
        for value in (corner, beside, over):
            came = swap(value[rows:], "tp")
            chip.append(value[:rows].astype(F32) + came.astype(F32))
        return chip

    def exchange(self, chip):
        corner, beside, over = chip
        half = corner.shape[0] // 2
        corner_x = swap(corner[:half].astype(BF), "ctx").astype(F32)
        corner_y = self.across(corner[half:].astype(BF)).astype(F32)
        own_x = swap(beside[:half].astype(BF), "ctx").astype(F32)
        own_y = self.across(over[half:].astype(BF)).astype(F32)
        last_y = self.across((over[:half] + corner_x).astype(BF)).astype(F32)
        last_x = swap((beside[half:] + corner_y).astype(BF), "ctx").astype(F32)
        return own_x, own_y, last_x, last_y

    def reduce_own(self, partial, far):
        rows = partial.shape[0] // 2
        own_x, own_y, last_x, last_y = far
        came = swap(partial[rows:], "tp")
        extra = jnp.concatenate([own_x + last_y, own_y + last_x], axis=0)
        return partial[:rows].astype(F32) + came.astype(F32) + extra


def swap(value, axis):
    return lax.ppermute(value, axis, [(0, 1), (1, 0)])


def gelu_parts(value):
    inner = 0.7978845608028654 * (value + 0.044715 * value * value * value)
    tanh = jnp.tanh(inner)
    slope = 0.7978845608028654 * (1.0 + 3.0 * 0.044715 * value * value)
    gelu = 0.5 * value * (1.0 + tanh)
    back = 0.5 * (1.0 + tanh) + 0.5 * value * (1.0 - tanh * tanh) * slope
    return gelu, back


def tied(value, *deps):
    return lax.optimization_barrier((value,) + deps)[0]


def shards(
    plane,
    inputs,
    gain_attn,
    w_query,
    w_key,
    w_value,
    w_out,
    bias_table,
    buckets,
    gain_ffn,
    w_gate,
    w_up,
    w_down,
    cotangent,
):
    seq_dev, tokens, width = inputs.shape
    block = tokens // 2
    length = 2 * tokens
    fsdp, ctx, tp = lax.axis_index("fsdp"), lax.axis_index("ctx"), lax.axis_index("tp")
    line, side = fsdp // 2, fsdp % 2
    me = side * 2 + ctx
    heads, ffn_cols = bias_table.shape[1] // 4, w_gate.shape[1] // 4

    def quarter(weight, which):
        count = weight.shape[1] // 4
        return lax.dynamic_slice_in_dim(weight, which * count, count, axis=1)

    def line_shard(weights, gain=None, after=None):
        def cut(which):
            pieces = [quarter(weight, which) for weight in weights]
            if gain is not None:
                factor = gain.astype(F32)[:, None]
                pieces = [(piece.astype(F32) * factor).astype(BF) for piece in pieces]
            return jnp.concatenate(pieces, axis=1)

        give = cut(jnp.bitwise_xor(me, 2))
        return plane.recut(cut(me), give if after is None else tied(give, after), side)

    order = [(line - step + plane.line) % plane.line for step in range(plane.line)]
    info = jnp.stack([tp] + order).astype(jnp.int32)
    square_info = jnp.stack([me, ctx]).astype(jnp.int32)
    pos = jnp.stack(
        [
            ((ctx + far) % 2) * tokens + ((tp + turn) % 2) * block
            for far in range(2)
            for turn in range(2)
        ]
    ).astype(jnp.int32)

    qkv_line = line_shard((w_query, w_key, w_value), gain_attn)
    qkv_pieces = plane.ring(qkv_line)
    qkv_full = jnp.concatenate(qkv_pieces, axis=0)
    kept, normed, grad_own = enter(info, inputs[0], cotangent[0])
    kept, grad_mine = kept[:block].astype(F32), grad_own[:block]
    normed = plane.share(tied(normed[:block], qkv_line), normed[block:])
    out_line = line_shard((w_out,), None, qkv_line)
    down_line = line_shard((w_down,), None, qkv_line)
    ffn_line = line_shard((w_gate, w_up), gain_ffn, qkv_line)
    grads = plane.share(tied(grad_mine, normed), grad_own[block:])

    table = lax.dynamic_slice_in_dim(bias_table, me * heads, heads, axis=1)
    reach = 2 * length
    reversed_buckets = jnp.pad(buckets[::-1], (0, 1), constant_values=-1)
    hits = (
        jnp.arange(bias_table.shape[0], dtype=jnp.int32)[:, None] == reversed_buckets[None, :]
    ).astype(F32)
    rows_rev = lax.dot_general(
        table.astype(F32),
        hits,
        TN,
        precision=lax.Precision.HIGHEST,
        preferred_element_type=F32,
    ).reshape(heads // 2, 2, reach)

    def project(left, weight):
        beyond = dot(left[length:], weight, NT, BF)
        within = dot(left[:length], weight, NT, BF)
        return within[:tokens], (within[tokens:], beyond[:tokens], beyond[tokens:])

    qkv = dot(normed, qkv_full, NN, BF)
    out_full = plane.pieces(tied(out_line, qkv_pieces[-2]), line, qkv)
    down_line, ffn_line = tied(down_line, qkv_pieces[-1]), tied(ffn_line, qkv_pieces[-1])
    attended = attention_forward(qkv, rows_rev, pos, block, length)
    down_full = plane.pieces(down_line, line, attended)
    ffn_full = plane.pieces(ffn_line, line, attended)
    own, rest = project(attended, out_full)
    far = plane.exchange(plane.chip_sums(*rest))
    grad_activ = dot(grads, down_full)
    hidden = kept + plane.reduce_own(own, far)

    rms_two = lax.rsqrt(jnp.mean(hidden * hidden, axis=-1, keepdims=True) + EPS)
    two = plane.share((hidden * rms_two).astype(BF))
    pre = dot(two, ffn_full)
    gate, up = pre[:, :ffn_cols], pre[:, ffn_cols:]
    gelu, back = gelu_parts(gate)
    activ = (gelu * up).astype(BF)
    both = jnp.concatenate(
        [(back * up * grad_activ).astype(BF), (gelu * grad_activ).astype(BF)], axis=1
    )

    own, rest = project(both, ffn_full)
    chip = plane.chip_sums(*rest)
    far = plane.exchange(chip)
    ffn_part = dot(two, tied(both, chip[0]), TN, BF)
    ffn_sums = plane.scatter(ffn_part)
    down_part = dot(grads, tied(activ, ffn_part), TN, BF)
    down_sums = plane.scatter(down_part)
    back_two = plane.reduce_own(own, far)
    grad_hidden = (
        grad_mine.astype(F32)
        + rms_two * back_two
        - hidden * rms_two**3 * jnp.mean(hidden * back_two, axis=-1, keepdims=True)
    )
    branch_mine = grad_hidden.astype(BF)
    branch = plane.share(branch_mine)

    result_own, rest = project(tied(activ, branch_mine), down_full)
    result_chip = plane.chip_sums(*rest)

    grad_attended = dot(branch, out_full, NN, BF)
    out_part = dot(branch, attended, TN, BF)
    out_sums = plane.scatter(out_part)
    *result_chip, _ = lax.optimization_barrier((*result_chip, grad_attended))
    result_far = plane.exchange(result_chip)
    grad_attended = tied(grad_attended, out_part, result_chip[0])
    grad_qkv, diag = attention_backward(qkv, grad_attended, rows_rev, pos, block, length)
    qkv_part = dot(normed, grad_qkv, TN, BF)
    qkv_sums = plane.scatter(qkv_part)
    own, rest = project(tied(grad_qkv, qkv_part), qkv_full)
    chip = plane.chip_sums(*rest)
    far = plane.exchange(chip)
    result = (hidden + plane.reduce_own(tied(result_own, chip[0]), result_far)).astype(BF)
    result = leave(info, result, swap(result, "tp"))
    back_one = plane.reduce_own(own, far)
    rms_one = lax.rsqrt(jnp.mean(kept * kept, axis=-1, keepdims=True) + EPS)
    input_grad = (
        grad_hidden
        + rms_one * back_one
        - kept * rms_one**3 * jnp.mean(kept * back_one, axis=-1, keepdims=True)
    ).astype(BF)
    input_grad = leave(info, input_grad, swap(input_grad, "tp"))

    def finish(sums, after, parts, weights=(), gain=None):
        *sums, _ = lax.optimization_barrier((*sums, after))
        total = sum(piece.astype(F32) for piece in sums)
        rows = total.shape[0] // 4
        pieces = [
            lax.dynamic_slice_in_dim(total, jnp.bitwise_xor(me, far) * rows, rows)
            for far in range(4)
        ]
        moved = plane.square([piece.astype(BF) for piece in pieces])
        if gain is not None:
            gain = gain.astype(F32)[:, None]
        found = settle(square_info, pieces[0], moved, weights, gain, parts)
        if gain is None:
            return found
        rest = found[parts][:, 0]
        return [*found[:parts], rest + swap(rest, "tp")]

    (down_grad,) = finish(down_sums, chip[0], 1)
    *ffn_grads, gain_ffn_grad = finish(ffn_sums, chip[0], 2, (w_gate, w_up), gain_ffn)
    (out_grad,) = finish(out_sums, chip[0], 1)
    *qkv_grads, gain_attn_grad = finish(qkv_sums, chip[0], 3, (w_query, w_key, w_value), gain_attn)

    diag = diag.reshape(heads, 8, reach)
    shifted = sum(jnp.roll(diag[:, row, :], 7 - row, axis=1) for row in range(8))
    table_part = lax.dot_general(
        hits, shifted, NT, precision=lax.Precision.HIGHEST, preferred_element_type=F32
    )
    table_part = sum(
        [plane.along(table_part, step) for step in range(1, plane.line)], start=table_part
    )
    one, two_away, three = plane.square([table_part] * 4)
    near = jnp.where(
        ctx == 0,
        jnp.concatenate([table_part, one, two_away, three], axis=1),
        jnp.concatenate([one, table_part, three, two_away], axis=1),
    )
    table_grad = jnp.where(side == 0, near, jnp.roll(near, 2 * heads, axis=1))

    return (
        result[None],
        input_grad[None],
        gain_attn_grad,
        *qkv_grads,
        out_grad,
        table_grad,
        gain_ffn_grad,
        *ffn_grads,
        down_grad,
    )


def solution(mesh):
    plane = Plane(mesh.shape["fsdp"])
    placed = (
        P("fsdp", "ctx", None),
        P("fsdp"),
        P("fsdp", "tp"),
        P("fsdp", "tp"),
        P("fsdp", "tp"),
        P("fsdp", "tp"),
        P(None, "tp"),
        P(),
        P("fsdp"),
        P("fsdp", "tp"),
        P("fsdp", "tp"),
        P("fsdp", "tp"),
        P("fsdp", "ctx", None),
    )
    rows = P(("fsdp", "ctx"))
    matrix = P(("fsdp", "ctx"), "tp")
    return jax.shard_map(
        functools.partial(shards, plane),
        mesh=mesh,
        in_specs=placed,
        out_specs=(
            P("fsdp", "ctx", None),
            P("fsdp", "ctx", None),
            rows,
            matrix,
            matrix,
            matrix,
            matrix,
            P(None, "tp"),
            rows,
            matrix,
            matrix,
            matrix,
        ),
        check_vma=False,
    )
```

```python
import functools

import jax
import jax.numpy as jnp
from jax import lax
from jax.experimental import pallas as pl
from jax.experimental.pallas import tpu as pltpu
from jax.sharding import PartitionSpec as P


DH = 64
EPS = 1e-06
LANES = 128
BF = jnp.bfloat16
F32 = jnp.float32
NT = (((1,), (1,)), ((), ()))
NN = (((1,), (0,)), ((), ()))
TN = (((0,), (0,)), ((), ()))


def dot(left, right, dims=NN, out=F32):
    return lax.dot_general(left, right, dims, preferred_element_type=F32).astype(out)


def fill_toeplitz(row, table_ref, head):
    span = row.shape[1]
    base = jnp.broadcast_to(row, (8, span))
    block = pltpu.roll(base, span - 7, 1, stride=1, stride_axis=0)
    count = 8
    while count < LANES:
        block = jnp.concatenate([pltpu.roll(block, span - count, 1), block], axis=0)
        count *= 2
    table_ref[head] = block


def bias_start(pos_ref, query_block, key_row, block, length):
    key_block = key_row // block
    start = pos_ref[query_block] - pos_ref[key_block] - (key_row - key_block * block)
    return pl.multiple_of(start + length - LANES, LANES)


def raw_scores(pos_ref, keys, query, table_ref, head, tile, block, length):
    scores = dot(keys, query, NT)
    parts = []
    for row in range(0, length, LANES):
        start = bias_start(pos_ref, tile, row, block, length)
        parts.append(scores[row : row + LANES, :] + table_ref[head, :, pl.ds(start, block)])
    return parts


def column_max(parts):
    top = parts[0]
    for part in parts[1:]:
        top = jnp.maximum(top, part)
    return jnp.max(top, axis=0, keepdims=True)


def column_sum(parts):
    total = parts[0]
    for part in parts[1:]:
        total = total + part
    return jnp.sum(total, axis=0, keepdims=True)


def forward_kernel(pos_ref, q_ref, k_ref, v_ref, row_ref, out_ref, table_ref, *, block):
    length = q_ref.shape[0]

    @pl.when(pl.program_id(1) == 0)
    def _():
        for head in range(2):
            fill_toeplitz(row_ref[0, head : head + 1, :], table_ref, head)

    keys = k_ref[...]
    values_t = v_ref[...].T
    low_lanes = lax.broadcasted_iota(jnp.int32, (block, LANES), 1) < DH
    for tile in range(length // block):
        spot = pl.ds(tile * block, block)
        query = q_ref[spot, :]
        mixed = []
        for head in range(2):
            mine = jnp.where(low_lanes == (head == 0), query, jnp.zeros_like(query))
            parts = raw_scores(pos_ref, keys, mine, table_ref, head, tile, block, length)
            top = column_max(parts)
            parts = [jnp.exp(part - top) for part in parts]
            scale = 1.0 / column_sum(parts)
            weight = jnp.concatenate([part.astype(BF) for part in parts], axis=0)
            mixed.append(dot(values_t[head * DH : (head + 1) * DH, :], weight) * scale)
        out_ref[spot, :] = jnp.concatenate(mixed, axis=0).T.astype(BF)


def backward_kernel(
    pos_ref,
    q_ref,
    k_ref,
    v_ref,
    d_ref,
    row_ref,
    grads_ref,
    diag_ref,
    table_ref,
    sums_ref,
    gk_ref,
    gv_ref,
    *,
    block,
):
    pair, seq = pl.program_id(0), pl.program_id(1)
    length = q_ref.shape[0]
    cols = grads_ref.shape[1] // 3

    @pl.when(seq == 0)
    def _():
        for head in range(2):
            fill_toeplitz(row_ref[0, head : head + 1, :], table_ref, head)
        sums_ref[...] = jnp.zeros_like(sums_ref)

    keys, values = k_ref[...], v_ref[...]
    keys_t = keys.T
    low_lanes = lax.broadcasted_iota(jnp.int32, (block, LANES), 1) < DH

    def place(start):
        return pl.ds(pl.multiple_of(start + pair * LANES, LANES), LANES)

    for tile in range(length // block):
        spot = pl.ds(tile * block, block)
        query, grad = q_ref[spot, :], d_ref[spot, :]
        mixed, key_part, value_part = [], None, None
        for head in range(2):
            pick = low_lanes == (head == 0)
            mine = jnp.where(pick, query, jnp.zeros_like(query))
            back = jnp.where(pick, grad, jnp.zeros_like(grad))
            parts = raw_scores(pos_ref, keys, mine, table_ref, head, tile, block, length)
            top = column_max(parts)
            parts = [jnp.exp(part - top) for part in parts]
            scale = 1.0 / column_sum(parts)
            parts = [part * scale for part in parts]
            probs_low = jnp.concatenate([part.astype(BF) for part in parts], axis=0)
            grad_probs = dot(values, back, NT)
            moved = [
                part * grad_probs[row * LANES : (row + 1) * LANES, :]
                for row, part in enumerate(parts)
            ]
            delta = column_sum(moved)
            moved = [both - part * delta for both, part in zip(moved, parts)]
            for row, part in enumerate(moved):
                start = bias_start(pos_ref, tile, row * LANES, block, length)
                where = (head, slice(None), pl.ds(start, block))
                sums_ref[where] = sums_ref[where] + part
            scores_low = jnp.concatenate([part.astype(BF) for part in moved], axis=0)
            mixed.append(dot(keys_t[head * DH : (head + 1) * DH, :], scores_low))
            gv, gk = dot(probs_low, back), dot(scores_low, mine)
            value_part = gv if value_part is None else value_part + gv
            key_part = gk if key_part is None else key_part + gk
        rows = pl.ds(pl.multiple_of(seq * length + tile * block, block), block)
        grads_ref[rows, place(0)] = jnp.concatenate(mixed, axis=0).T.astype(BF)
        if tile:
            gk_ref[...] += key_part
            gv_ref[...] += value_part
        else:
            gk_ref[...] = key_part
            gv_ref[...] = value_part
    rows = pl.ds(pl.multiple_of(seq * length, length), length)
    grads_ref[rows, place(cols)] = gk_ref[...].astype(BF)
    grads_ref[rows, place(2 * cols)] = gv_ref[...].astype(BF)

    @pl.when(seq == pl.num_programs(1) - 1)
    def _():
        for head in range(2):
            folded = sums_ref[head]
            count = LANES // 2
            while count >= 8:
                folded = pltpu.roll(folded[:count], count, 1) + folded[count:]
                count //= 2
            diag_ref[0, head] = folded


def attention_specs(length, pairs, span):
    def column(offset):
        return pl.BlockSpec((length, LANES), lambda p, e, pos, o=offset: (e, o * pairs + p))

    row = pl.BlockSpec((1, 2, span), lambda p, e, pos: (p, 0, 0))
    return column, [column(part) for part in range(3)], row


def attention_forward(qkv, rows_rev, pos, block, length):
    rows, width = qkv.shape
    cols = width // 3
    pairs, span = cols // LANES, rows_rev.shape[2]
    column, specs, row = attention_specs(length, pairs, span)
    return pl.pallas_call(
        functools.partial(forward_kernel, block=block),
        out_shape=jax.ShapeDtypeStruct((rows, cols), BF),
        grid_spec=pltpu.PrefetchScalarGridSpec(
            num_scalar_prefetch=1,
            grid=(pairs, rows // length),
            in_specs=specs + [row],
            out_specs=column(0),
            scratch_shapes=[pltpu.VMEM((2, LANES, span), F32)],
        ),
        compiler_params=pltpu.CompilerParams(vmem_limit_bytes=40 << 20),
        cost_estimate=pl.CostEstimate(
            flops=16 * length * rows * cols,
            bytes_accessed=8 * rows * cols,
            transcendentals=length * rows * cols // DH,
        ),
        name="attend",
    )(pos, qkv, qkv, qkv, rows_rev)


def attention_backward(qkv, grad, rows_rev, pos, block, length):
    rows, width = qkv.shape
    cols = width // 3
    pairs, span = cols // LANES, rows_rev.shape[2]
    column, specs, row = attention_specs(length, pairs, span)
    return pl.pallas_call(
        functools.partial(backward_kernel, block=block),
        out_shape=(
            jax.ShapeDtypeStruct((rows, width), BF),
            jax.ShapeDtypeStruct((pairs, 2, 8, span), F32),
        ),
        grid_spec=pltpu.PrefetchScalarGridSpec(
            num_scalar_prefetch=1,
            grid=(pairs, rows // length),
            in_specs=specs + [column(0), row],
            out_specs=(
                pl.BlockSpec((rows, width), lambda p, e, pos: (0, 0)),
                pl.BlockSpec((1, 2, 8, span), lambda p, e, pos: (p, 0, 0, 0)),
            ),
            scratch_shapes=[
                pltpu.VMEM((2, LANES, span), F32),
                pltpu.VMEM((2, LANES, span), F32),
                pltpu.VMEM((length, LANES), F32),
                pltpu.VMEM((length, LANES), F32),
            ],
        ),
        compiler_params=pltpu.CompilerParams(vmem_limit_bytes=48 << 20),
        cost_estimate=pl.CostEstimate(
            flops=40 * length * rows * cols,
            bytes_accessed=16 * rows * cols,
            transcendentals=length * rows * cols // DH,
        ),
        name="attend_back",
    )(pos, qkv, qkv, qkv, grad, rows_rev)


def enter_kernel(info_ref, in_ref, cot_ref, kept_ref, normed_ref, grad_ref):
    blocks = info_ref.shape[0] - 1
    step = in_ref.shape[1] // blocks
    value = in_ref[...].astype(F32)
    scale = lax.rsqrt(jnp.mean(value * value, axis=-1, keepdims=True) + EPS)
    for index in range(blocks):
        source = pl.ds(pl.multiple_of(info_ref[index + 1] * step, step), step)
        target = pl.ds(index * step, step)
        piece = in_ref[:, source]
        kept_ref[:, target] = piece
        normed_ref[:, target] = (piece.astype(F32) * scale).astype(BF)
        grad_ref[:, target] = cot_ref[:, source]


def enter(info, inputs, cotangent):
    rows, width = inputs.shape
    spec_in = pl.BlockSpec((rows // 2, width), lambda r, info: (jnp.bitwise_xor(r, info[0]), 0))
    spec_out = pl.BlockSpec((rows // 2, width), lambda r, info: (r, 0))
    shape = jax.ShapeDtypeStruct((rows, width), BF)
    return pl.pallas_call(
        enter_kernel,
        out_shape=(shape, shape, shape),
        grid_spec=pltpu.PrefetchScalarGridSpec(
            num_scalar_prefetch=1,
            grid=(2,),
            in_specs=[spec_in, spec_in],
            out_specs=(spec_out,) * 3,
        ),
        name="enter",
    )(info, inputs, cotangent)


def leave_kernel(info_ref, mine_ref, other_ref, out_ref):
    blocks = info_ref.shape[0] - 1
    rows = mine_ref.shape[0]
    step = mine_ref.shape[1] // blocks
    first = pl.ds(pl.multiple_of(info_ref[0] * rows, rows), rows)
    second = pl.ds(pl.multiple_of((1 - info_ref[0]) * rows, rows), rows)
    for index in range(blocks):
        target = pl.ds(pl.multiple_of(info_ref[index + 1] * step, step), step)
        source = pl.ds(index * step, step)
        out_ref[first, target] = mine_ref[:, source]
        out_ref[second, target] = other_ref[:, source]


def leave(info, mine, other):
    rows, width = mine.shape
    spec = pl.BlockSpec((rows, width), lambda r, info: (0, 0))
    return pl.pallas_call(
        leave_kernel,
        out_shape=jax.ShapeDtypeStruct((2 * rows, width), BF),
        grid_spec=pltpu.PrefetchScalarGridSpec(
            num_scalar_prefetch=1,
            grid=(1,),
            in_specs=[spec, spec],
            out_specs=pl.BlockSpec((2 * rows, width), lambda r, info: (0, 0)),
        ),
        name="leave",
    )(info, mine, other)


def settle_kernel(info_ref, keep_ref, *refs, parts, scaled):
    moved, refs = refs[:3], refs[3:]
    weights, refs = (refs[:parts], refs[parts:]) if scaled else ((), refs)
    gain_ref, refs = (refs[0], refs[1:]) if scaled else (None, refs)
    outs = refs[:parts]
    cols = keep_ref.shape[1] // parts
    total = None
    for far in range(4):
        place = pl.multiple_of(jnp.bitwise_xor(info_ref[0], far) * cols, LANES)
        for part in range(parts):
            source = pl.ds(part * cols, cols)
            piece = keep_ref[:, source] if far == 0 else moved[far - 1][:, source].astype(F32)
            if scaled:
                weight = weights[part][:, pl.ds(place, cols)].astype(F32)
                along = jnp.sum(piece * weight, axis=1, keepdims=True)
                total = along if total is None else total + along
                piece = piece * gain_ref[...]
            outs[part][:, pl.ds(place, cols)] = piece
    if scaled:
        refs[parts][...] = jnp.broadcast_to(total, refs[parts].shape)


def settle(info, keep, moved, weights, gain, parts):
    rows, width = keep.shape
    cols = 4 * width // parts
    same = pl.BlockSpec((rows, width), lambda i, info: (0, 0))
    half = pl.BlockSpec((rows, cols), lambda i, info: (jnp.bitwise_and(info[0], 1), 0))
    out_spec = pl.BlockSpec((rows, cols), lambda i, info: (0, 0))
    scaled = gain is not None
    operands = [keep, *moved]
    specs = [same] * 4
    out_specs = [out_spec] * parts
    shapes = [jax.ShapeDtypeStruct((rows, cols), F32)] * parts
    if scaled:
        operands += [*weights, gain]
        specs += [half] * parts
        specs += [pl.BlockSpec((rows, 1), lambda i, info: (jnp.bitwise_and(info[0], 1), 0))]
        out_specs += [pl.BlockSpec((rows, LANES), lambda i, info: (0, 0))]
        shapes += [jax.ShapeDtypeStruct((rows, LANES), F32)]
    return pl.pallas_call(
        functools.partial(settle_kernel, parts=parts, scaled=scaled),
        out_shape=shapes,
        grid_spec=pltpu.PrefetchScalarGridSpec(
            num_scalar_prefetch=1, grid=(1,), in_specs=specs, out_specs=out_specs
        ),
        name="settle",
    )(info, *operands)


class Plane:
    def __init__(self, count):
        self.count = count
        self.line = count // 2

    def permute(self, value, move):
        pairs = []
        for index in range(self.count):
            target = move(index // 2, index % 2)
            if target is not None:
                pairs.append((index, target[0] * 2 + target[1]))
        return lax.ppermute(value, "fsdp", pairs)

    def along(self, value, step):
        return self.permute(value, lambda z, y: ((z + step) % self.line, y))

    def hop(self, value, moves):
        return self.permute(value, lambda z, y: (moves[z], y) if z in moves else None)

    def across(self, value):
        return self.permute(value, lambda z, y: (z, 1 - y))

    def diagonal(self, value):
        pairs = []
        for index in range(self.count):
            for side in range(2):
                pairs.append((index * 2 + side, (index ^ 1) * 2 + 1 - side))
        return lax.ppermute(value, ("fsdp", "ctx"), pairs)

    def square(self, pieces):
        return [swap(pieces[1], "ctx"), self.across(pieces[2]), self.diagonal(pieces[3])]

    def recut(self, mine, theirs, side):
        came = self.across(theirs)
        return jnp.where(
            side == 0,
            jnp.concatenate([mine, came], axis=0),
            jnp.concatenate([came, mine], axis=0),
        )

    def ring(self, shard):
        pieces = [shard]
        for _ in range(self.line - 1):
            pieces.append(self.along(pieces[-1], 1))
        return pieces

    def pieces(self, shard, place, after):
        if self.line != 4:
            found = [shard] + [self.along(shard, step) for step in range(1, self.line)]
            return jnp.concatenate(found, axis=0)
        two = self.along(shard, 2)
        up = self.hop(shard, {0: 1, 1: 2, 2: 3})
        down = self.hop(shard, {1: 0, 2: 1, 3: 2})
        two, up, down, _ = lax.optimization_barrier((two, up, down, after))
        far = self.hop(two, {1: 0, 2: 3})
        found = [shard, jnp.where(place == 0, far, up), two, jnp.where(place == 3, far, down)]
        return jnp.concatenate(found, axis=0)

    def scatter(self, whole):
        rows = whole.shape[0] // self.line
        sent = [
            self.along(whole[step * rows : (step + 1) * rows], -step)
            for step in range(1, self.line)
        ]
        return whole[:rows], *sent

    def share(self, mine, partner=None):
        half = mine.shape[0] // 2
        partner = swap(mine, "tp") if partner is None else partner
        beside = swap(mine, "ctx")
        over = self.across(mine)
        corner = jnp.concatenate([swap(over[:half], "ctx"), self.across(beside[half:])], axis=0)
        return jnp.concatenate(
            [
                mine,
                partner,
                beside,
                swap(beside, "tp"),
                over,
                swap(over, "tp"),
                corner,
                swap(corner, "tp"),
            ],
            axis=0,
        )

    def chip_sums(self, beside, over, corner):
        rows = beside.shape[0] // 2
        chip = []
        for value in (corner, beside, over):
            came = swap(value[rows:], "tp")
            chip.append(value[:rows].astype(F32) + came.astype(F32))
        return chip

    def exchange(self, chip):
        corner, beside, over = chip
        half = corner.shape[0] // 2
        corner_x = swap(corner[:half].astype(BF), "ctx").astype(F32)
        corner_y = self.across(corner[half:].astype(BF)).astype(F32)
        own_x = swap(beside[:half].astype(BF), "ctx").astype(F32)
        own_y = self.across(over[half:].astype(BF)).astype(F32)
        last_y = self.across((over[:half] + corner_x).astype(BF)).astype(F32)
        last_x = swap((beside[half:] + corner_y).astype(BF), "ctx").astype(F32)
        return own_x, own_y, last_x, last_y

    def reduce_own(self, partial, far):
        rows = partial.shape[0] // 2
        own_x, own_y, last_x, last_y = far
        came = swap(partial[rows:], "tp")
        extra = jnp.concatenate([own_x + last_y, own_y + last_x], axis=0)
        return partial[:rows].astype(F32) + came.astype(F32) + extra


def swap(value, axis):
    return lax.ppermute(value, axis, [(0, 1), (1, 0)])


def gelu_parts(value):
    inner = 0.7978845608028654 * (value + 0.044715 * value * value * value)
    tanh = jnp.tanh(inner)
    slope = 0.7978845608028654 * (1.0 + 3.0 * 0.044715 * value * value)
    gelu = 0.5 * value * (1.0 + tanh)
    back = 0.5 * (1.0 + tanh) + 0.5 * value * (1.0 - tanh * tanh) * slope
    return gelu, back


def tied(value, *deps):
    return lax.optimization_barrier((value,) + deps)[0]


def shards(
    plane,
    inputs,
    gain_attn,
    w_query,
    w_key,
    w_value,
    w_out,
    bias_table,
    buckets,
    gain_ffn,
    w_gate,
    w_up,
    w_down,
    cotangent,
):
    seq_dev, tokens, width = inputs.shape
    block = tokens // 2
    length = 2 * tokens
    fsdp, ctx, tp = lax.axis_index("fsdp"), lax.axis_index("ctx"), lax.axis_index("tp")
    line, side = fsdp // 2, fsdp % 2
    me = side * 2 + ctx
    heads, ffn_cols = bias_table.shape[1] // 4, w_gate.shape[1] // 4

    def quarter(weight, which):
        count = weight.shape[1] // 4
        return lax.dynamic_slice_in_dim(weight, which * count, count, axis=1)

    def line_shard(weights, gain=None, after=None):
        def cut(which):
            pieces = [quarter(weight, which) for weight in weights]
            if gain is not None:
                factor = gain.astype(F32)[:, None]
                pieces = [(piece.astype(F32) * factor).astype(BF) for piece in pieces]
            return jnp.concatenate(pieces, axis=1)

        give = cut(jnp.bitwise_xor(me, 2))
        return plane.recut(cut(me), give if after is None else tied(give, after), side)

    order = [(line - step + plane.line) % plane.line for step in range(plane.line)]
    info = jnp.stack([tp] + order).astype(jnp.int32)
    square_info = jnp.stack([me, ctx]).astype(jnp.int32)
    pos = jnp.stack(
        [
            ((ctx + far) % 2) * tokens + ((tp + turn) % 2) * block
            for far in range(2)
            for turn in range(2)
        ]
    ).astype(jnp.int32)

    qkv_line = line_shard((w_query, w_key, w_value), gain_attn)
    qkv_pieces = plane.ring(qkv_line)
    qkv_full = jnp.concatenate(qkv_pieces, axis=0)
    kept, normed, grad_own = enter(info, inputs[0], cotangent[0])
    kept, grad_mine = kept[:block].astype(F32), grad_own[:block]
    normed = plane.share(tied(normed[:block], qkv_line), normed[block:])
    out_line = line_shard((w_out,), None, qkv_line)
    down_line = line_shard((w_down,), None, qkv_line)
    ffn_line = line_shard((w_gate, w_up), gain_ffn, qkv_line)
    grads = plane.share(tied(grad_mine, normed), grad_own[block:])

    table = lax.dynamic_slice_in_dim(bias_table, me * heads, heads, axis=1)
    reach = 2 * length
    reversed_buckets = jnp.pad(buckets[::-1], (0, 1), constant_values=-1)
    hits = (
        jnp.arange(bias_table.shape[0], dtype=jnp.int32)[:, None] == reversed_buckets[None, :]
    ).astype(F32)
    rows_rev = lax.dot_general(
        table.astype(F32),
        hits,
        TN,
        precision=lax.Precision.HIGHEST,
        preferred_element_type=F32,
    ).reshape(heads // 2, 2, reach)

    def project(left, weight):
        beyond = dot(left[length:], weight, NT, BF)
        within = dot(left[:length], weight, NT, BF)
        return within[:tokens], (within[tokens:], beyond[:tokens], beyond[tokens:])

    qkv = dot(normed, qkv_full, NN, BF)
    out_full = plane.pieces(tied(out_line, qkv_pieces[-2]), line, qkv)
    down_line, ffn_line = tied(down_line, qkv_pieces[-1]), tied(ffn_line, qkv_pieces[-1])
    attended = attention_forward(qkv, rows_rev, pos, block, length)
    ffn_full = plane.pieces(ffn_line, line, attended)
    own, rest = project(attended, out_full)
    chip = plane.chip_sums(*rest)
    far = plane.exchange(chip)
    down_full = plane.pieces(down_line, line, chip[0])
    grad_activ = dot(grads, down_full)
    hidden = kept + plane.reduce_own(own, far)

    rms_two = lax.rsqrt(jnp.mean(hidden * hidden, axis=-1, keepdims=True) + EPS)
    two = plane.share((hidden * rms_two).astype(BF))
    pre = dot(two, ffn_full)
    gate, up = pre[:, :ffn_cols], pre[:, ffn_cols:]
    gelu, back = gelu_parts(gate)
    activ = (gelu * up).astype(BF)
    both = jnp.concatenate(
        [(back * up * grad_activ).astype(BF), (gelu * grad_activ).astype(BF)], axis=1
    )

    own, rest = project(both, ffn_full)
    chip = plane.chip_sums(*rest)
    far = plane.exchange(chip)
    ffn_part = dot(two, tied(both, chip[0]), TN, BF)
    ffn_sums = plane.scatter(ffn_part)
    down_part = dot(grads, tied(activ, ffn_part), TN, BF)
    down_sums = plane.scatter(down_part)
    back_two = plane.reduce_own(own, far)
    grad_hidden = (
        grad_mine.astype(F32)
        + rms_two * back_two
        - hidden * rms_two**3 * jnp.mean(hidden * back_two, axis=-1, keepdims=True)
    )
    branch_mine = grad_hidden.astype(BF)
    branch = plane.share(branch_mine)

    result_own, rest = project(tied(activ, branch_mine), down_full)
    result_chip = plane.chip_sums(*rest)

    grad_attended = dot(branch, out_full, NN, BF)
    out_part = dot(branch, attended, TN, BF)
    out_sums = plane.scatter(out_part)
    *result_chip, _ = lax.optimization_barrier((*result_chip, grad_attended))
    result_far = plane.exchange(result_chip)
    grad_attended = tied(grad_attended, out_part, result_chip[0])
    grad_qkv, diag = attention_backward(qkv, grad_attended, rows_rev, pos, block, length)
    qkv_part = dot(normed, grad_qkv, TN, BF)
    qkv_sums = plane.scatter(qkv_part)
    own, rest = project(tied(grad_qkv, qkv_part), qkv_full)
    chip = plane.chip_sums(*rest)
    far = plane.exchange(chip)
    result = (hidden + plane.reduce_own(tied(result_own, chip[0]), result_far)).astype(BF)
    result = leave(info, result, swap(result, "tp"))
    back_one = plane.reduce_own(own, far)
    rms_one = lax.rsqrt(jnp.mean(kept * kept, axis=-1, keepdims=True) + EPS)
    input_grad = (
        grad_hidden
        + rms_one * back_one
        - kept * rms_one**3 * jnp.mean(kept * back_one, axis=-1, keepdims=True)
    ).astype(BF)
    input_grad = leave(info, input_grad, swap(input_grad, "tp"))

    def finish(sums, after, parts, weights=(), gain=None):
        *sums, _ = lax.optimization_barrier((*sums, after))
        total = sum(piece.astype(F32) for piece in sums)
        rows = total.shape[0] // 4
        pieces = [
            lax.dynamic_slice_in_dim(total, jnp.bitwise_xor(me, far) * rows, rows)
            for far in range(4)
        ]
        moved = plane.square([piece.astype(BF) for piece in pieces])
        if gain is not None:
            gain = gain.astype(F32)[:, None]
        found = settle(square_info, pieces[0], moved, weights, gain, parts)
        if gain is None:
            return found
        rest = found[parts][:, 0]
        return [*found[:parts], rest + swap(rest, "tp")]

    (down_grad,) = finish(down_sums, chip[0], 1)
    *ffn_grads, gain_ffn_grad = finish(ffn_sums, chip[0], 2, (w_gate, w_up), gain_ffn)
    (out_grad,) = finish(out_sums, chip[0], 1)
    *qkv_grads, gain_attn_grad = finish(qkv_sums, chip[0], 3, (w_query, w_key, w_value), gain_attn)

    diag = diag.reshape(heads, 8, reach)
    shifted = sum(jnp.roll(diag[:, row, :], 7 - row, axis=1) for row in range(8))
    table_part = lax.dot_general(
        hits, shifted, NT, precision=lax.Precision.HIGHEST, preferred_element_type=F32
    )
    table_part = sum(
        [plane.along(table_part, step) for step in range(1, plane.line)], start=table_part
    )
    one, two_away, three = plane.square([table_part] * 4)
    near = jnp.where(
        ctx == 0,
        jnp.concatenate([table_part, one, two_away, three], axis=1),
        jnp.concatenate([one, table_part, three, two_away], axis=1),
    )
    table_grad = jnp.where(side == 0, near, jnp.roll(near, 2 * heads, axis=1))

    return (
        result[None],
        input_grad[None],
        gain_attn_grad,
        *qkv_grads,
        out_grad,
        table_grad,
        gain_ffn_grad,
        *ffn_grads,
        down_grad,
    )


def solution(mesh):
    plane = Plane(mesh.shape["fsdp"])
    placed = (
        P("fsdp", "ctx", None),
        P("fsdp"),
        P("fsdp", "tp"),
        P("fsdp", "tp"),
        P("fsdp", "tp"),
        P("fsdp", "tp"),
        P(None, "tp"),
        P(),
        P("fsdp"),
        P("fsdp", "tp"),
        P("fsdp", "tp"),
        P("fsdp", "tp"),
        P("fsdp", "ctx", None),
    )
    rows = P(("fsdp", "ctx"))
    matrix = P(("fsdp", "ctx"), "tp")
    return jax.shard_map(
        functools.partial(shards, plane),
        mesh=mesh,
        in_specs=placed,
        out_specs=(
            P("fsdp", "ctx", None),
            P("fsdp", "ctx", None),
            rows,
            matrix,
            matrix,
            matrix,
            matrix,
            P(None, "tp"),
            rows,
            matrix,
            matrix,
            matrix,
        ),
        check_vma=False,
    )
```

```python
import functools

import jax
import jax.numpy as jnp
from jax import lax
from jax.experimental import pallas as pl
from jax.experimental.pallas import tpu as pltpu
from jax.sharding import PartitionSpec as P


DH = 64
EPS = 1e-06
LANES = 128
BF = jnp.bfloat16
F32 = jnp.float32
NT = (((1,), (1,)), ((), ()))
NN = (((1,), (0,)), ((), ()))
TN = (((0,), (0,)), ((), ()))


def dot(left, right, dims=NN, out=F32):
    return lax.dot_general(left, right, dims, preferred_element_type=F32).astype(out)


def fill_toeplitz(row, table_ref, head):
    span = row.shape[1]
    base = jnp.broadcast_to(row, (8, span))
    block = pltpu.roll(base, span - 7, 1, stride=1, stride_axis=0)
    count = 8
    while count < LANES:
        block = jnp.concatenate([pltpu.roll(block, span - count, 1), block], axis=0)
        count *= 2
    table_ref[head] = block


def bias_start(pos_ref, query_block, key_row, block, length):
    key_block = key_row // block
    start = pos_ref[query_block] - pos_ref[key_block] - (key_row - key_block * block)
    return pl.multiple_of(start + length - LANES, LANES)


def raw_scores(pos_ref, keys, query, table_ref, head, tile, block, length):
    scores = dot(keys, query, NT)
    parts = []
    for row in range(0, length, LANES):
        start = bias_start(pos_ref, tile, row, block, length)
        parts.append(scores[row : row + LANES, :] + table_ref[head, :, pl.ds(start, block)])
    return parts


def column_max(parts):
    top = parts[0]
    for part in parts[1:]:
        top = jnp.maximum(top, part)
    return jnp.max(top, axis=0, keepdims=True)


def column_sum(parts):
    total = parts[0]
    for part in parts[1:]:
        total = total + part
    return jnp.sum(total, axis=0, keepdims=True)


def forward_kernel(pos_ref, q_ref, k_ref, v_ref, row_ref, out_ref, table_ref, *, block):
    length = q_ref.shape[0]

    @pl.when(pl.program_id(1) == 0)
    def _():
        for head in range(2):
            fill_toeplitz(row_ref[0, head : head + 1, :], table_ref, head)

    keys = k_ref[...]
    values_t = v_ref[...].T
    low_lanes = lax.broadcasted_iota(jnp.int32, (block, LANES), 1) < DH
    for tile in range(length // block):
        spot = pl.ds(tile * block, block)
        query = q_ref[spot, :]
        mixed = []
        for head in range(2):
            mine = jnp.where(low_lanes == (head == 0), query, jnp.zeros_like(query))
            parts = raw_scores(pos_ref, keys, mine, table_ref, head, tile, block, length)
            top = column_max(parts)
            parts = [jnp.exp(part - top) for part in parts]
            scale = 1.0 / column_sum(parts)
            weight = jnp.concatenate([part.astype(BF) for part in parts], axis=0)
            mixed.append(dot(values_t[head * DH : (head + 1) * DH, :], weight) * scale)
        out_ref[spot, :] = jnp.concatenate(mixed, axis=0).T.astype(BF)


def backward_kernel(
    pos_ref,
    q_ref,
    k_ref,
    v_ref,
    d_ref,
    row_ref,
    grads_ref,
    diag_ref,
    table_ref,
    sums_ref,
    gk_ref,
    gv_ref,
    *,
    block,
):
    pair, seq = pl.program_id(0), pl.program_id(1)
    length = q_ref.shape[0]
    cols = grads_ref.shape[1] // 3

    @pl.when(seq == 0)
    def _():
        for head in range(2):
            fill_toeplitz(row_ref[0, head : head + 1, :], table_ref, head)
        sums_ref[...] = jnp.zeros_like(sums_ref)

    keys, values = k_ref[...], v_ref[...]
    keys_t = keys.T
    low_lanes = lax.broadcasted_iota(jnp.int32, (block, LANES), 1) < DH

    def place(start):
        return pl.ds(pl.multiple_of(start + pair * LANES, LANES), LANES)

    for tile in range(length // block):
        spot = pl.ds(tile * block, block)
        query, grad = q_ref[spot, :], d_ref[spot, :]
        mixed, key_part, value_part = [], None, None
        for head in range(2):
            pick = low_lanes == (head == 0)
            mine = jnp.where(pick, query, jnp.zeros_like(query))
            back = jnp.where(pick, grad, jnp.zeros_like(grad))
            parts = raw_scores(pos_ref, keys, mine, table_ref, head, tile, block, length)
            top = column_max(parts)
            parts = [jnp.exp(part - top) for part in parts]
            scale = 1.0 / column_sum(parts)
            parts = [part * scale for part in parts]
            probs_low = jnp.concatenate([part.astype(BF) for part in parts], axis=0)
            grad_probs = dot(values, back, NT)
            moved = [
                part * grad_probs[row * LANES : (row + 1) * LANES, :]
                for row, part in enumerate(parts)
            ]
            delta = column_sum(moved)
            moved = [both - part * delta for both, part in zip(moved, parts)]
            for row, part in enumerate(moved):
                start = bias_start(pos_ref, tile, row * LANES, block, length)
                where = (head, slice(None), pl.ds(start, block))
                sums_ref[where] = sums_ref[where] + part
            scores_low = jnp.concatenate([part.astype(BF) for part in moved], axis=0)
            mixed.append(dot(keys_t[head * DH : (head + 1) * DH, :], scores_low))
            gv, gk = dot(probs_low, back), dot(scores_low, mine)
            value_part = gv if value_part is None else value_part + gv
            key_part = gk if key_part is None else key_part + gk
        rows = pl.ds(pl.multiple_of(seq * length + tile * block, block), block)
        grads_ref[rows, place(0)] = jnp.concatenate(mixed, axis=0).T.astype(BF)
        if tile:
            gk_ref[...] += key_part
            gv_ref[...] += value_part
        else:
            gk_ref[...] = key_part
            gv_ref[...] = value_part
    rows = pl.ds(pl.multiple_of(seq * length, length), length)
    grads_ref[rows, place(cols)] = gk_ref[...].astype(BF)
    grads_ref[rows, place(2 * cols)] = gv_ref[...].astype(BF)

    @pl.when(seq == pl.num_programs(1) - 1)
    def _():
        for head in range(2):
            folded = sums_ref[head]
            count = LANES // 2
            while count >= 8:
                folded = pltpu.roll(folded[:count], count, 1) + folded[count:]
                count //= 2
            diag_ref[0, head] = folded


def attention_specs(length, pairs, span):
    def column(offset):
        return pl.BlockSpec((length, LANES), lambda p, e, pos, o=offset: (e, o * pairs + p))

    row = pl.BlockSpec((1, 2, span), lambda p, e, pos: (p, 0, 0))
    return column, [column(part) for part in range(3)], row


def attention_forward(qkv, rows_rev, pos, block, length):
    rows, width = qkv.shape
    cols = width // 3
    pairs, span = cols // LANES, rows_rev.shape[2]
    column, specs, row = attention_specs(length, pairs, span)
    return pl.pallas_call(
        functools.partial(forward_kernel, block=block),
        out_shape=jax.ShapeDtypeStruct((rows, cols), BF),
        grid_spec=pltpu.PrefetchScalarGridSpec(
            num_scalar_prefetch=1,
            grid=(pairs, rows // length),
            in_specs=specs + [row],
            out_specs=column(0),
            scratch_shapes=[pltpu.VMEM((2, LANES, span), F32)],
        ),
        compiler_params=pltpu.CompilerParams(vmem_limit_bytes=40 << 20),
        cost_estimate=pl.CostEstimate(
            flops=16 * length * rows * cols,
            bytes_accessed=8 * rows * cols,
            transcendentals=length * rows * cols // DH,
        ),
        name="attend",
    )(pos, qkv, qkv, qkv, rows_rev)


def attention_backward(qkv, grad, rows_rev, pos, block, length):
    rows, width = qkv.shape
    cols = width // 3
    pairs, span = cols // LANES, rows_rev.shape[2]
    column, specs, row = attention_specs(length, pairs, span)
    return pl.pallas_call(
        functools.partial(backward_kernel, block=block),
        out_shape=(
            jax.ShapeDtypeStruct((rows, width), BF),
            jax.ShapeDtypeStruct((pairs, 2, 8, span), F32),
        ),
        grid_spec=pltpu.PrefetchScalarGridSpec(
            num_scalar_prefetch=1,
            grid=(pairs, rows // length),
            in_specs=specs + [column(0), row],
            out_specs=(
                pl.BlockSpec((rows, width), lambda p, e, pos: (0, 0)),
                pl.BlockSpec((1, 2, 8, span), lambda p, e, pos: (p, 0, 0, 0)),
            ),
            scratch_shapes=[
                pltpu.VMEM((2, LANES, span), F32),
                pltpu.VMEM((2, LANES, span), F32),
                pltpu.VMEM((length, LANES), F32),
                pltpu.VMEM((length, LANES), F32),
            ],
        ),
        compiler_params=pltpu.CompilerParams(vmem_limit_bytes=48 << 20),
        cost_estimate=pl.CostEstimate(
            flops=40 * length * rows * cols,
            bytes_accessed=16 * rows * cols,
            transcendentals=length * rows * cols // DH,
        ),
        name="attend_back",
    )(pos, qkv, qkv, qkv, grad, rows_rev)


def enter_kernel(info_ref, in_ref, cot_ref, kept_ref, normed_ref, grad_ref):
    blocks = info_ref.shape[0] - 1
    step = in_ref.shape[1] // blocks
    value = in_ref[...].astype(F32)
    scale = lax.rsqrt(jnp.mean(value * value, axis=-1, keepdims=True) + EPS)
    for index in range(blocks):
        source = pl.ds(pl.multiple_of(info_ref[index + 1] * step, step), step)
        target = pl.ds(index * step, step)
        piece = in_ref[:, source]
        kept_ref[:, target] = piece
        normed_ref[:, target] = (piece.astype(F32) * scale).astype(BF)
        grad_ref[:, target] = cot_ref[:, source]


def enter(info, inputs, cotangent):
    rows, width = inputs.shape
    spec_in = pl.BlockSpec((rows // 2, width), lambda r, info: (jnp.bitwise_xor(r, info[0]), 0))
    spec_out = pl.BlockSpec((rows // 2, width), lambda r, info: (r, 0))
    shape = jax.ShapeDtypeStruct((rows, width), BF)
    return pl.pallas_call(
        enter_kernel,
        out_shape=(shape, shape, shape),
        grid_spec=pltpu.PrefetchScalarGridSpec(
            num_scalar_prefetch=1,
            grid=(2,),
            in_specs=[spec_in, spec_in],
            out_specs=(spec_out,) * 3,
        ),
        name="enter",
    )(info, inputs, cotangent)


def leave_kernel(info_ref, mine_ref, other_ref, out_ref):
    blocks = info_ref.shape[0] - 1
    rows = mine_ref.shape[0]
    step = mine_ref.shape[1] // blocks
    first = pl.ds(pl.multiple_of(info_ref[0] * rows, rows), rows)
    second = pl.ds(pl.multiple_of((1 - info_ref[0]) * rows, rows), rows)
    for index in range(blocks):
        target = pl.ds(pl.multiple_of(info_ref[index + 1] * step, step), step)
        source = pl.ds(index * step, step)
        out_ref[first, target] = mine_ref[:, source]
        out_ref[second, target] = other_ref[:, source]


def leave(info, mine, other):
    rows, width = mine.shape
    spec = pl.BlockSpec((rows, width), lambda r, info: (0, 0))
    return pl.pallas_call(
        leave_kernel,
        out_shape=jax.ShapeDtypeStruct((2 * rows, width), BF),
        grid_spec=pltpu.PrefetchScalarGridSpec(
            num_scalar_prefetch=1,
            grid=(1,),
            in_specs=[spec, spec],
            out_specs=pl.BlockSpec((2 * rows, width), lambda r, info: (0, 0)),
        ),
        name="leave",
    )(info, mine, other)


def settle_kernel(info_ref, keep_ref, *refs, parts, scaled):
    moved, refs = refs[:3], refs[3:]
    weights, refs = (refs[:parts], refs[parts:]) if scaled else ((), refs)
    gain_ref, refs = (refs[0], refs[1:]) if scaled else (None, refs)
    outs = refs[:parts]
    cols = keep_ref.shape[1] // parts
    total = None
    for far in range(4):
        place = pl.multiple_of(jnp.bitwise_xor(info_ref[0], far) * cols, LANES)
        for part in range(parts):
            source = pl.ds(part * cols, cols)
            piece = keep_ref[:, source] if far == 0 else moved[far - 1][:, source].astype(F32)
            if scaled:
                weight = weights[part][:, pl.ds(place, cols)].astype(F32)
                along = jnp.sum(piece * weight, axis=1, keepdims=True)
                total = along if total is None else total + along
                piece = piece * gain_ref[...]
            outs[part][:, pl.ds(place, cols)] = piece
    if scaled:
        refs[parts][...] = jnp.broadcast_to(total, refs[parts].shape)


def settle(info, keep, moved, weights, gain, parts):
    rows, width = keep.shape
    cols = 4 * width // parts
    same = pl.BlockSpec((rows, width), lambda i, info: (0, 0))
    half = pl.BlockSpec((rows, cols), lambda i, info: (jnp.bitwise_and(info[0], 1), 0))
    out_spec = pl.BlockSpec((rows, cols), lambda i, info: (0, 0))
    scaled = gain is not None
    operands = [keep, *moved]
    specs = [same] * 4
    out_specs = [out_spec] * parts
    shapes = [jax.ShapeDtypeStruct((rows, cols), F32)] * parts
    if scaled:
        operands += [*weights, gain]
        specs += [half] * parts
        specs += [pl.BlockSpec((rows, 1), lambda i, info: (jnp.bitwise_and(info[0], 1), 0))]
        out_specs += [pl.BlockSpec((rows, LANES), lambda i, info: (0, 0))]
        shapes += [jax.ShapeDtypeStruct((rows, LANES), F32)]
    return pl.pallas_call(
        functools.partial(settle_kernel, parts=parts, scaled=scaled),
        out_shape=shapes,
        grid_spec=pltpu.PrefetchScalarGridSpec(
            num_scalar_prefetch=1, grid=(1,), in_specs=specs, out_specs=out_specs
        ),
        name="settle",
    )(info, *operands)


class Plane:
    def __init__(self, count):
        self.count = count
        self.line = count // 2

    def permute(self, value, move):
        pairs = []
        for index in range(self.count):
            target = move(index // 2, index % 2)
            if target is not None:
                pairs.append((index, target[0] * 2 + target[1]))
        return lax.ppermute(value, "fsdp", pairs)

    def along(self, value, step):
        return self.permute(value, lambda z, y: ((z + step) % self.line, y))

    def hop(self, value, moves):
        return self.permute(value, lambda z, y: (moves[z], y) if z in moves else None)

    def across(self, value):
        return self.permute(value, lambda z, y: (z, 1 - y))

    def diagonal(self, value):
        pairs = []
        for index in range(self.count):
            for side in range(2):
                pairs.append((index * 2 + side, (index ^ 1) * 2 + 1 - side))
        return lax.ppermute(value, ("fsdp", "ctx"), pairs)

    def square(self, pieces):
        return [swap(pieces[1], "ctx"), self.across(pieces[2]), self.diagonal(pieces[3])]

    def recut(self, mine, theirs, side):
        came = self.across(theirs)
        return jnp.where(
            side == 0,
            jnp.concatenate([mine, came], axis=0),
            jnp.concatenate([came, mine], axis=0),
        )

    def ring(self, shard):
        pieces = [shard]
        for _ in range(self.line - 1):
            pieces.append(self.along(pieces[-1], 1))
        return pieces

    def pieces(self, shard, place, after):
        if self.line != 4:
            found = [shard] + [self.along(shard, step) for step in range(1, self.line)]
            return jnp.concatenate(found, axis=0)
        two = self.along(shard, 2)
        up = self.hop(shard, {0: 1, 1: 2, 2: 3})
        down = self.hop(shard, {1: 0, 2: 1, 3: 2})
        two, up, down, _ = lax.optimization_barrier((two, up, down, after))
        far = self.hop(two, {1: 0, 2: 3})
        found = [shard, jnp.where(place == 0, far, up), two, jnp.where(place == 3, far, down)]
        return jnp.concatenate(found, axis=0)

    def scatter(self, whole):
        rows = whole.shape[0] // self.line
        sent = [
            self.along(whole[step * rows : (step + 1) * rows], -step)
            for step in range(1, self.line)
        ]
        return whole[:rows], *sent

    def share(self, mine, partner=None):
        half = mine.shape[0] // 2
        partner = swap(mine, "tp") if partner is None else partner
        beside = swap(mine, "ctx")
        over = self.across(mine)
        corner = jnp.concatenate([swap(over[:half], "ctx"), self.across(beside[half:])], axis=0)
        return jnp.concatenate(
            [
                mine,
                partner,
                beside,
                swap(beside, "tp"),
                over,
                swap(over, "tp"),
                corner,
                swap(corner, "tp"),
            ],
            axis=0,
        )

    def chip_sums(self, beside, over, corner):
        rows = beside.shape[0] // 2
        chip = []
        for value in (corner, beside, over):
            came = swap(value[rows:], "tp")
            chip.append(value[:rows].astype(F32) + came.astype(F32))
        return chip

    def exchange(self, chip):
        corner, beside, over = chip
        half = corner.shape[0] // 2
        corner_x = swap(corner[:half].astype(BF), "ctx").astype(F32)
        corner_y = self.across(corner[half:].astype(BF)).astype(F32)
        own_x = swap(beside[:half].astype(BF), "ctx").astype(F32)
        own_y = self.across(over[half:].astype(BF)).astype(F32)
        last_y = self.across((over[:half] + corner_x).astype(BF)).astype(F32)
        last_x = swap((beside[half:] + corner_y).astype(BF), "ctx").astype(F32)
        return own_x, own_y, last_x, last_y

    def reduce_own(self, partial, far):
        rows = partial.shape[0] // 2
        own_x, own_y, last_x, last_y = far
        came = swap(partial[rows:], "tp")
        extra = jnp.concatenate([own_x + last_y, own_y + last_x], axis=0)
        return partial[:rows].astype(F32) + came.astype(F32) + extra


def swap(value, axis):
    return lax.ppermute(value, axis, [(0, 1), (1, 0)])


def gelu_parts(value):
    inner = 0.7978845608028654 * (value + 0.044715 * value * value * value)
    tanh = jnp.tanh(inner)
    slope = 0.7978845608028654 * (1.0 + 3.0 * 0.044715 * value * value)
    gelu = 0.5 * value * (1.0 + tanh)
    back = 0.5 * (1.0 + tanh) + 0.5 * value * (1.0 - tanh * tanh) * slope
    return gelu, back


def tied(value, *deps):
    return lax.optimization_barrier((value,) + deps)[0]


def shards(
    plane,
    inputs,
    gain_attn,
    w_query,
    w_key,
    w_value,
    w_out,
    bias_table,
    buckets,
    gain_ffn,
    w_gate,
    w_up,
    w_down,
    cotangent,
):
    seq_dev, tokens, width = inputs.shape
    block = tokens // 2
    length = 2 * tokens
    fsdp, ctx, tp = lax.axis_index("fsdp"), lax.axis_index("ctx"), lax.axis_index("tp")
    line, side = fsdp // 2, fsdp % 2
    me = side * 2 + ctx
    heads, ffn_cols = bias_table.shape[1] // 4, w_gate.shape[1] // 4

    def quarter(weight, which):
        count = weight.shape[1] // 4
        return lax.dynamic_slice_in_dim(weight, which * count, count, axis=1)

    def line_shard(weights, gain=None, after=None):
        def cut(which):
            pieces = [quarter(weight, which) for weight in weights]
            if gain is not None:
                factor = gain.astype(F32)[:, None]
                pieces = [(piece.astype(F32) * factor).astype(BF) for piece in pieces]
            return jnp.concatenate(pieces, axis=1)

        give = cut(jnp.bitwise_xor(me, 2))
        return plane.recut(cut(me), give if after is None else tied(give, after), side)

    order = [(line - step + plane.line) % plane.line for step in range(plane.line)]
    info = jnp.stack([tp] + order).astype(jnp.int32)
    square_info = jnp.stack([me, ctx]).astype(jnp.int32)
    pos = jnp.stack(
        [
            ((ctx + far) % 2) * tokens + ((tp + turn) % 2) * block
            for far in range(2)
            for turn in range(2)
        ]
    ).astype(jnp.int32)

    qkv_line = line_shard((w_query, w_key, w_value), gain_attn)
    qkv_pieces = plane.ring(qkv_line)
    qkv_full = jnp.concatenate(qkv_pieces, axis=0)
    kept, normed, grad_own = enter(info, inputs[0], cotangent[0])
    kept, grad_mine = kept[:block].astype(F32), grad_own[:block]
    normed = plane.share(tied(normed[:block], qkv_line), normed[block:])
    out_line = line_shard((w_out,), None, qkv_line)
    down_line = line_shard((w_down,), None, qkv_line)
    ffn_line = line_shard((w_gate, w_up), gain_ffn, qkv_line)
    grads = plane.share(tied(grad_mine, normed), grad_own[block:])

    table = lax.dynamic_slice_in_dim(bias_table, me * heads, heads, axis=1)
    reach = 2 * length
    reversed_buckets = jnp.pad(buckets[::-1], (0, 1), constant_values=-1)
    hits = (
        jnp.arange(bias_table.shape[0], dtype=jnp.int32)[:, None] == reversed_buckets[None, :]
    ).astype(F32)
    rows_rev = lax.dot_general(
        table.astype(F32),
        hits,
        TN,
        precision=lax.Precision.HIGHEST,
        preferred_element_type=F32,
    ).reshape(heads // 2, 2, reach)

    def project(left, weight):
        beyond = dot(left[length:], weight, NT, BF)
        within = dot(left[:length], weight, NT, BF)
        return within[:tokens], (within[tokens:], beyond[:tokens], beyond[tokens:])

    qkv = dot(normed, qkv_full, NN, BF)
    out_full = plane.pieces(tied(out_line, qkv_pieces[-2]), line, qkv)
    down_line, ffn_line = tied(down_line, qkv_pieces[-1]), tied(ffn_line, qkv_pieces[-1])
    attended = attention_forward(qkv, rows_rev, pos, block, length)
    down_full = plane.pieces(down_line, line, attended)
    ffn_full = plane.pieces(ffn_line, line, attended)
    own, rest = project(attended, out_full)
    far = plane.exchange(plane.chip_sums(*rest))
    grad_activ = dot(grads, down_full)
    hidden = kept + plane.reduce_own(own, far)

    rms_two = lax.rsqrt(jnp.mean(hidden * hidden, axis=-1, keepdims=True) + EPS)
    two = plane.share((hidden * rms_two).astype(BF))
    pre = dot(two, ffn_full)
    gate, up = pre[:, :ffn_cols], pre[:, ffn_cols:]
    gelu, back = gelu_parts(gate)
    activ = (gelu * up).astype(BF)
    both = jnp.concatenate(
        [(back * up * grad_activ).astype(BF), (gelu * grad_activ).astype(BF)], axis=1
    )

    down_part = dot(grads, activ, TN, BF)
    down_sums = plane.scatter(down_part)
    own, rest = project(tied(both, down_part), ffn_full)
    chip = plane.chip_sums(*rest)
    far = plane.exchange(chip)
    ffn_part = dot(two, tied(both, chip[0]), TN, BF)
    ffn_sums = plane.scatter(ffn_part)
    back_two = plane.reduce_own(own, far)
    grad_hidden = (
        grad_mine.astype(F32)
        + rms_two * back_two
        - hidden * rms_two**3 * jnp.mean(hidden * back_two, axis=-1, keepdims=True)
    )
    branch_mine = grad_hidden.astype(BF)
    branch = plane.share(branch_mine)

    result_own, rest = project(tied(activ, branch_mine), down_full)
    result_chip = plane.chip_sums(*rest)

    grad_attended = dot(branch, out_full, NN, BF)
    out_part = dot(branch, attended, TN, BF)
    out_sums = plane.scatter(out_part)
    *result_chip, _ = lax.optimization_barrier((*result_chip, grad_attended))
    result_far = plane.exchange(result_chip)
    grad_attended = tied(grad_attended, out_part, result_chip[0])
    grad_qkv, diag = attention_backward(qkv, grad_attended, rows_rev, pos, block, length)
    qkv_part = dot(normed, grad_qkv, TN, BF)
    qkv_sums = plane.scatter(qkv_part)
    own, rest = project(tied(grad_qkv, qkv_part), qkv_full)
    chip = plane.chip_sums(*rest)
    far = plane.exchange(chip)
    result = (hidden + plane.reduce_own(tied(result_own, chip[0]), result_far)).astype(BF)
    result = leave(info, result, swap(result, "tp"))
    back_one = plane.reduce_own(own, far)
    rms_one = lax.rsqrt(jnp.mean(kept * kept, axis=-1, keepdims=True) + EPS)
    input_grad = (
        grad_hidden
        + rms_one * back_one
        - kept * rms_one**3 * jnp.mean(kept * back_one, axis=-1, keepdims=True)
    ).astype(BF)
    input_grad = leave(info, input_grad, swap(input_grad, "tp"))

    def finish(sums, after, parts, weights=(), gain=None):
        *sums, _ = lax.optimization_barrier((*sums, after))
        total = sum(piece.astype(F32) for piece in sums)
        rows = total.shape[0] // 4
        pieces = [
            lax.dynamic_slice_in_dim(total, jnp.bitwise_xor(me, far) * rows, rows)
            for far in range(4)
        ]
        moved = plane.square([piece.astype(BF) for piece in pieces])
        if gain is not None:
            gain = gain.astype(F32)[:, None]
        found = settle(square_info, pieces[0], moved, weights, gain, parts)
        if gain is None:
            return found
        rest = found[parts][:, 0]
        return [*found[:parts], rest + swap(rest, "tp")]

    (down_grad,) = finish(down_sums, chip[0], 1)
    *ffn_grads, gain_ffn_grad = finish(ffn_sums, chip[0], 2, (w_gate, w_up), gain_ffn)
    (out_grad,) = finish(out_sums, chip[0], 1)
    *qkv_grads, gain_attn_grad = finish(qkv_sums, chip[0], 3, (w_query, w_key, w_value), gain_attn)

    diag = diag.reshape(heads, 8, reach)
    shifted = sum(jnp.roll(diag[:, row, :], 7 - row, axis=1) for row in range(8))
    table_part = lax.dot_general(
        hits, shifted, NT, precision=lax.Precision.HIGHEST, preferred_element_type=F32
    )
    table_part = sum(
        [plane.along(table_part, step) for step in range(1, plane.line)], start=table_part
    )
    one, two_away, three = plane.square([table_part] * 4)
    near = jnp.where(
        ctx == 0,
        jnp.concatenate([table_part, one, two_away, three], axis=1),
        jnp.concatenate([one, table_part, three, two_away], axis=1),
    )
    table_grad = jnp.where(side == 0, near, jnp.roll(near, 2 * heads, axis=1))

    return (
        result[None],
        input_grad[None],
        gain_attn_grad,
        *qkv_grads,
        out_grad,
        table_grad,
        gain_ffn_grad,
        *ffn_grads,
        down_grad,
    )


def solution(mesh):
    plane = Plane(mesh.shape["fsdp"])
    placed = (
        P("fsdp", "ctx", None),
        P("fsdp"),
        P("fsdp", "tp"),
        P("fsdp", "tp"),
        P("fsdp", "tp"),
        P("fsdp", "tp"),
        P(None, "tp"),
        P(),
        P("fsdp"),
        P("fsdp", "tp"),
        P("fsdp", "tp"),
        P("fsdp", "tp"),
        P("fsdp", "ctx", None),
    )
    rows = P(("fsdp", "ctx"))
    matrix = P(("fsdp", "ctx"), "tp")
    return jax.shard_map(
        functools.partial(shards, plane),
        mesh=mesh,
        in_specs=placed,
        out_specs=(
            P("fsdp", "ctx", None),
            P("fsdp", "ctx", None),
            rows,
            matrix,
            matrix,
            matrix,
            matrix,
            P(None, "tp"),
            rows,
            matrix,
            matrix,
            matrix,
        ),
        check_vma=False,
    )
```
